512 devices in a mesh: tok: 32 (over z_hi, y, core), feat: 16 (over x, z_lo).
Axes of the slice: x: 4, y: 4, z: 16 (z_hi: 4, z_lo: 4; z = z_hi * 4 + z_lo), core: 2. Of those that a mesh axis runs over, the one named last changes fastest.
Arguments:
- calib: float32 [5120, 28672], P('tok', 'feat'), may hold values from -6 to 6
- weight: float32 [28672, 512], P('feat', 'tok'), may hold values from -0.03125 to 0.03125
Outputs:
- gram_product: float32 [512, 28672], P('tok', 'feat')
The draws below stay inside these ranges and needn't reach their ends.
All inputs are finite; a program needn't handle non-finite values.
Results may differ from the reference program's by a relative error of at most 0.000098.
Values sent between devices are 32-bit elements; how exact they have to be, the bound alone decides.
A program may use at most 64 MiB of HBM per device.

```python
import math
import jax
import jax.numpy as jnp
from jax import lax

F = 28672
C = 512
TOKENS = 5120


def block_scale(stream_key, extent, shards, smallest, largest):
    def one(axis_at, shards_of):
        draws = jax.random.uniform(jax.random.fold_in(jax.random.fold_in(stream_key, 6), axis_at), (shards_of,), jnp.float32, smallest / len(shards), largest / len(shards))
        return jnp.repeat(jnp.exp(draws), extent[axis_at] // shards_of).reshape((-1,) + (1,) * (len(extent) - axis_at - 1))

    level = one(*shards[0])
    for cut in shards[1:]:
        level = level * one(*cut)
    return level


def gaussian(own_key, shape, scale, reach, cuts=(), kind=jnp.bfloat16):
    result = jax.random.normal(own_key, shape, jnp.float32) * scale
    if len(cuts) > 0:
        result = block_scale(own_key, shape, cuts, -0.22, 0.18) * result
    return jnp.clip(result, min=-reach, max=reach).astype(kind)


def setup_inputs(seed: int = 0) -> dict:
    splits = jax.random.split(jax.random.key(seed), 3)
    calib = gaussian(splits[0], (TOKENS, F), 1.0, 6.0, ((0, 32), (1, 16)), jnp.float32)
    weight = gaussian(splits[1], (F, C), F ** -0.5, 0.03125, ((0, 16), (1, 32)), jnp.float32)
    return dict(calib=calib, weight=weight)


def reference(calib, weight):
    mixed = jnp.dot(calib, weight, precision=lax.Precision.HIGHEST, preferred_element_type=jnp.float32)
    gram = lax.dot_general(mixed, calib, (((0,), (0,)), ((), ())), precision=lax.Precision.HIGHEST, preferred_element_type=jnp.float32)
    return gram * (1.0 / math.sqrt(TOKENS))
```

```python
import functools
import math

import jax
import jax.numpy as jnp
from jax import lax
from jax.experimental import pallas as pl
from jax.experimental.pallas import tpu as pltpu
from jax.sharding import PartitionSpec as P

MESH = pl.DeviceIdType.MESH
NZ, NY, NC, NX, NL = 4, 4, 2, 4, 4
NP = NX * NC
ORDER = (0, 2, 1, 3)


def split(v):
    hi = v.astype(jnp.bfloat16)
    return hi, (v - hi.astype(jnp.float32)).astype(jnp.bfloat16)


def dot3(a, b, dims):
    (ah, al), (bh, bl) = a, b
    f = lambda p, q: lax.dot_general(
        p, q, (dims, ((), ())), preferred_element_type=jnp.float32
    )
    return f(ah, bh) + (f(ah, bl) + f(al, bh))


def kernel(
    factor,
    calib,
    wt,
    out,
    a,
    ah,
    al,
    g,
    p,
    rs,
    zx,
    m,
    yo,
    yr,
    rz,
    zr,
    loc_sem,
    a_send,
    a_recv,
    w_send,
    w_recv,
    gy_send,
    gy_recv,
    rs_send,
    rs_recv,
    zx_send,
    zx_recv,
    m_send,
    m_recv,
    yr_send,
    yr_recv,
    zr_send,
    zr_recv,
):
    tok, feat = lax.axis_index("tok"), lax.axis_index("feat")
    zh, y, c = tok // (NY * NC), lax.rem(tok, NY * NC) // NC, lax.rem(tok, NC)
    x, zl = feat // NL, lax.rem(feat, NL)
    pm = x * NC + c
    half = calib.shape[1] // NC
    rows = calib.shape[0]
    wide = wt.shape[0]

    def dev(zh=zh, y=y, c=c, x=x, zl=zl):
        return ((zh * NY + y) * NC + c, x * NL + zl)

    def along_z(j, core):
        return dev(zh=lax.rem(zh + j, NZ), c=core)

    def along_y(j):
        return dev(y=lax.rem(y + j, NY))

    def along_l(j):
        return dev(zl=lax.rem(zl + j, NL))

    def piece(j):
        q = lax.rem(pm + j, NP)
        return q, dev(x=q // NC, c=lax.rem(q, NC))

    partner = dev(c=1 - c)

    def send(src, dst, ssem, rsem, to):
        pltpu.make_async_remote_copy(
            src_ref=src,
            dst_ref=dst,
            send_sem=ssem,
            recv_sem=rsem,
            device_id=to,
            device_id_type=MESH,
        ).start()

    def await_bytes(ref, sem):
        pltpu.make_async_copy(ref, ref, sem).wait()

    mine = pl.ds(pl.multiple_of(c * half, 128), half)
    theirs = pl.ds(pl.multiple_of((1 - c) * half, 128), half)
    my_rows = pl.ds(pl.multiple_of(c * rows, 8), rows)
    my_wide = pl.ds(pl.multiple_of(c * wide, 8), wide)

    a_own = pltpu.make_async_copy(calib.at[:, mine], a.at[my_rows], loc_sem.at[0])
    w_own = pltpu.make_async_copy(wt.at[:, mine], g.at[0, y, my_wide], loc_sem.at[1])
    w_own.start()
    a_own.start()

    barrier = pltpu.get_barrier_semaphore()

    def greet(to):
        pl.semaphore_signal(barrier, inc=1, device_id=to, device_id_type=MESH)

    for j in range(1, NZ):
        for k in range(NC):
            greet(along_z(j, k))
    for j in range(1, NY):
        greet(along_y(j))
    for j in range(1, NL):
        greet(along_l(j))
    for j in range(1, NP):
        greet(piece(j)[1])
    pl.semaphore_wait(barrier, (NZ - 1) * NC + (NY - 1) + (NL - 1) + (NP - 1))

    send(wt.at[:, theirs], g.at[0, y, my_wide], w_send.at[0], w_recv.at[0], partner)
    for j in (2, 1, 3):
        for k in range(NC):
            send(
                wt.at[:, pl.ds(k * half, half)],
                g.at[NZ - j, y, my_wide],
                w_send.at[j],
                w_recv.at[NZ - j],
                along_z(j, k),
            )
    send(calib.at[:, theirs], a.at[my_rows], a_send, a_recv, partner)

    def forward(d):
        if d == 0:
            w_own.wait()
            await_bytes(g.at[0, y, my_wide], w_recv.at[0])
        else:
            await_bytes(g.at[d, y], w_recv.at[d])
        for j in range(1, NY):
            send(g.at[d, y], g.at[d, y], gy_send.at[d], gy_recv.at[d], along_y(j))

    def s1(d):
        await_bytes(g.at[d, pl.ds(0, NY - 1)], gy_recv.at[d])
        w = split(g[d].reshape(NY * NC * wide, half))
        acc = dot3((ah[...], al[...]), w, ((1,), (1,)))
        p[d] = acc.reshape(p.shape[1:])

        def one(j, _):
            q, to = piece(j)
            send(p.at[d, q], rs.at[d, j - 1], rs_send.at[d], rs_recv.at[d], to)
            return 0

        lax.fori_loop(1, NP, one, 0)

    def s2(d):
        await_bytes(rs.at[d], rs_recv.at[d])
        acc = p[d, pm]
        for j in range(NP - 1):
            acc = acc + rs[d, j]
        zx[d, zl] = acc
        for j in range(1, NL):
            send(zx.at[d, zl], zx.at[d, zl], zx_send.at[d], zx_recv.at[d], along_l(j))

    def s3(d):
        await_bytes(zx.at[d, pl.ds(0, NL - 1)], zx_recv.at[d])
        acc = zx[d, 0]
        for j in range(1, NL):
            acc = acc + zx[d, j]
        m[d, pm] = acc * factor

        def one(j, _):
            send(m.at[d, pm], m.at[d, pm], m_send.at[d], m_recv.at[d], piece(j)[1])
            return 0

        lax.fori_loop(1, NP, one, 0)

    def s4(d):
        await_bytes(m.at[d, pl.ds(0, NP - 1)], m_recv.at[d])
        v = split(m[d].reshape(NC * rows, NY * NC * wide))
        acc = dot3(v, (ah[...], al[...]), ((0,), (0,)))
        yo[d] = acc.reshape(yo.shape[1:])
        for j in range(1, NY):
            send(
                yo.at[d, lax.rem(y + j, NY)],
                yr.at[d, j - 1],
                yr_send.at[d],
                yr_recv.at[d],
                along_y(j),
            )

    def s5(d):
        await_bytes(yr.at[d], yr_recv.at[d])
        acc = yo[d, y]
        for j in range(NY - 1):
            acc = acc + yr[d, j]
        rz[d] = acc.reshape(rz.shape[1:])
        if d == 0:
            send(rz.at[0, 1 - c], zr.at[0, c], zr_send.at[0], zr_recv.at[0], partner)
        else:
            for k in range(NC):
                send(
                    rz.at[d, k],
                    zr.at[d, c],
                    zr_send.at[d],
                    zr_recv.at[d],
                    along_z(d, k),
                )

    forward(0)
    a_own.wait()
    await_bytes(a.at[my_rows], a_recv)
    hi, lo = split(a[...])
    ah[...] = hi
    al[...] = lo
    s1(0)
    s2(0)
    forward(2)
    forward(1)
    s3(0)
    forward(3)
    s1(2)
    s4(0)
    s1(1)
    s2(2)
    s1(3)
    s2(1)
    s5(0)
    s3(2)
    s2(3)
    s4(2)
    s3(1)
    s4(1)
    s3(3)
    s5(2)
    s4(3)
    s5(1)
    s5(3)

    zr[0, c] = rz[0, c]
    await_bytes(zr.at[0, 0], zr_recv.at[0])
    for d in range(1, NZ):
        await_bytes(zr.at[d], zr_recv.at[d])
    for k in range(NC):
        acc = zr[0, k]
        for d in range(1, NZ):
            acc = acc + zr[d, k]
        out[:, k * half : (k + 1) * half] = acc

    await_bytes(a.at[my_rows], a_send)
    await_bytes(g.at[0, y, my_wide], w_send.at[0])
    await_bytes(zr.at[0, 0], zr_send.at[0])
    for d in range(NZ):
        if d:
            await_bytes(g.at[d, y], w_send.at[d])
            await_bytes(zr.at[d], zr_send.at[d])
        await_bytes(g.at[d, pl.ds(0, NY - 1)], gy_send.at[d])
        await_bytes(rs.at[d], rs_send.at[d])
        await_bytes(zx.at[d, pl.ds(0, NL - 1)], zx_send.at[d])
        await_bytes(m.at[d, pl.ds(0, NP - 1)], m_send.at[d])
        await_bytes(yr.at[d], yr_send.at[d])


def shards(calib, weight):
    rows, feats = calib.shape
    wide = weight.shape[1]
    half = feats // NC
    part = NC * rows // NP
    f32, bf16 = jnp.float32, jnp.bfloat16
    cols = NY * NC * wide
    factor = 1.0 / math.sqrt(rows * lax.axis_size("tok"))
    dma = lambda *n: pltpu.SemaphoreType.DMA(n)
    return pl.pallas_call(
        functools.partial(kernel, factor),
        out_shape=jax.ShapeDtypeStruct((wide, feats), f32),
        in_specs=[pl.BlockSpec(memory_space=pl.ANY)] * 2,
        out_specs=pl.BlockSpec(memory_space=pltpu.VMEM),
        scratch_shapes=[
            pltpu.VMEM((NC * rows, half), f32),
            pltpu.VMEM((NC * rows, half), bf16),
            pltpu.VMEM((NC * rows, half), bf16),
            pltpu.VMEM((NZ, NY, NC * wide, half), f32),
            pltpu.VMEM((NZ, NP, part, cols), f32),
            pltpu.VMEM((NZ, NP - 1, part, cols), f32),
            pltpu.VMEM((NZ, NL, part, cols), f32),
            pltpu.VMEM((NZ, NP, part, cols), f32),
            pltpu.VMEM((NZ, NY, NC * wide, half), f32),
            pltpu.VMEM((NZ, NY - 1, NC * wide, half), f32),
            pltpu.VMEM((NZ, NC, wide, half), f32),
            pltpu.VMEM((NZ, NC, wide, half), f32),
            dma(2),
            pltpu.SemaphoreType.DMA,
            pltpu.SemaphoreType.DMA,
            *[dma(NZ) for _ in range(14)],
        ],
        compiler_params=pltpu.CompilerParams(
            collective_id=0,
            has_side_effects=True,
            vmem_limit_bytes=48 * 1024 * 1024,
        ),
        name="gram",
    )(calib, weight.T)


def solution(mesh):
    return jax.shard_map(
        shards,
        mesh=mesh,
        in_specs=(P("tok", "feat"), P("feat", "tok")),
        out_specs=P("tok", "feat"),
        check_vma=False,
    )
```

```python
import functools
import math

import jax
import jax.numpy as jnp
from jax import lax
from jax.experimental import pallas as pl
from jax.experimental.pallas import tpu as pltpu
from jax.sharding import PartitionSpec as P

MESH = pl.DeviceIdType.MESH
NZ, NY, NC, NX, NL = 4, 4, 2, 4, 4
NP = NX * NC
SUB = 8


STEPS = (
    (0, 0), (0, 1), (1, 0), (0, 2), (1, 1), (2, 0), (0, 3), (1, 2),
    (2, 1), (3, 0), (1, 3), (2, 2), (3, 1), (4, 0), (2, 3), (3, 2),
    (4, 1), (5, 0), (3, 3), (4, 2), (5, 1), (4, 3), (5, 2), (5, 3),
)


def split(v):
    hi = v.astype(jnp.bfloat16)
    return hi, (v - hi.astype(jnp.float32)).astype(jnp.bfloat16)


def dot3(a, b, dims):
    (ah, al), (bh, bl) = a, b
    f = lambda p, q: lax.dot_general(
        p, q, (dims, ((), ())), preferred_element_type=jnp.float32
    )
    return f(ah, bh) + (f(ah, bl) + f(al, bh))


def kernel(
    factor,
    calib,
    wt,
    out,
    a,
    ah,
    al,
    g,
    p,
    rs,
    zx,
    m,
    yo,
    yr,
    rz,
    zr,
    loc_sem,
    a_send,
    a_recv,
    wp_send,
    wp_recv,
    go_send,
    go_recv,
    w_send,
    w_recv,
    gy_send,
    gy_recv,
    rs_send,
    rs_recv,
    zx_send,
    zx_recv,
    m_send,
    m_recv,
    yr_send,
    yr_recv,
    zr_send,
    zp_send,
    zr_recv,
):
    tok, feat = lax.axis_index("tok"), lax.axis_index("feat")
    zh, y, c = tok // (NY * NC), lax.rem(tok, NY * NC) // NC, lax.rem(tok, NC)
    x, zl = feat // NL, lax.rem(feat, NL)
    pm = x * NC + c
    half = calib.shape[1] // NC
    rows = calib.shape[0]
    per = wt.shape[0]
    chunks = NC * per

    def dev(zh=zh, y=y, c=c, x=x, zl=zl):
        return ((zh * NY + y) * NC + c, x * NL + zl)

    def along_z(j, core):
        return dev(zh=lax.rem(zh + j, NZ), c=core)

    def along_y(j):
        return dev(y=lax.rem(y + j, NY))

    def along_l(j):
        return dev(zl=lax.rem(zl + j, NL))

    def piece(j):
        q = lax.rem(pm + j, NP)
        return q, dev(x=q // NC, c=lax.rem(q, NC))

    partner = dev(c=1 - c)

    def send(src, dst, ssem, rsem, to):
        pltpu.make_async_remote_copy(
            src_ref=src,
            dst_ref=dst,
            send_sem=ssem,
            recv_sem=rsem,
            device_id=to,
            device_id_type=MESH,
        ).start()

    def await_bytes(ref, sem):
        pltpu.make_async_copy(ref, ref, sem).wait()

    mine = pl.ds(pl.multiple_of(c * half, 128), half)
    theirs = pl.ds(pl.multiple_of((1 - c) * half, 128), half)
    my_rows = pl.ds(pl.multiple_of(c * rows, 8), rows)
    my_chunks = pl.ds(c * per, per)

    a_own = pltpu.make_async_copy(calib.at[:, mine], a.at[my_rows], loc_sem.at[0])
    w_own = pltpu.make_async_copy(
        wt.at[:, :, mine], g.at[my_chunks, y, 0], loc_sem.at[1]
    )
    w_own.start()
    a_own.start()

    barrier = pltpu.get_barrier_semaphore()

    def greet(to):
        pl.semaphore_signal(barrier, inc=1, device_id=to, device_id_type=MESH)

    for j in range(1, NZ):
        for k in range(NC):
            greet(along_z(j, k))
    for j in range(1, NY):
        greet(along_y(j))
    for j in range(1, NL):
        greet(along_l(j))
    for j in range(1, NP):
        greet(piece(j)[1])
    pl.semaphore_wait(barrier, (NZ - 1) * NC + (NY - 1) + (NL - 1) + (NP - 1))

    send(wt.at[:, :, theirs], g.at[my_chunks, y, 0], wp_send, wp_recv, partner)
    w_own.wait()
    await_bytes(g.at[my_chunks, y, 0], wp_recv)
    for q in range(chunks):
        for j in (2, 1, 3):
            send(
                g.at[q, y, 0],
                g.at[q, y, NZ - j],
                w_send.at[q],
                w_recv.at[q],
                along_z(j, c),
            )
    for j in range(1, NY):
        send(g.at[:, y, 0], g.at[:, y, 0], go_send, go_recv, along_y(j))
    send(calib.at[:, theirs], a.at[my_rows], a_send, a_recv, partner)

    def forward(q):
        got = g.at[q, y, pl.ds(1, NZ - 1)]
        await_bytes(got, w_recv.at[q])
        for j in range(1, NY):
            send(got, got, gy_send.at[q], gy_recv.at[q], along_y(j))

    def s1(q):
        if q == 0:
            await_bytes(g.at[0, pl.ds(0, NY - 1)], go_recv)
        await_bytes(g.at[q, pl.ds(0, NY - 1), pl.ds(0, NZ - 1)], gy_recv.at[q])
        w = split(g[q].reshape(NY * NZ * SUB, half))
        acc = dot3((ah[...], al[...]), w, ((1,), (1,)))
        p[q] = acc.reshape(p.shape[1:])

        def one(j, _):
            t, to = piece(j)
            send(p.at[q, t], rs.at[q, j - 1], rs_send.at[q], rs_recv.at[q], to)
            return 0

        lax.fori_loop(1, NP, one, 0)

    def s2(q):
        await_bytes(rs.at[q], rs_recv.at[q])
        acc = p[q, pm]
        for j in range(NP - 1):
            acc = acc + rs[q, j]
        zx[q, zl] = acc
        for j in range(1, NL):
            send(zx.at[q, zl], zx.at[q, zl], zx_send.at[q], zx_recv.at[q], along_l(j))

    def s3(q):
        await_bytes(zx.at[q, pl.ds(0, NL - 1)], zx_recv.at[q])
        acc = zx[q, 0]
        for j in range(1, NL):
            acc = acc + zx[q, j]
        m[q, pm] = acc * factor

        def one(j, _):
            send(m.at[q, pm], m.at[q, pm], m_send.at[q], m_recv.at[q], piece(j)[1])
            return 0

        lax.fori_loop(1, NP, one, 0)

    def s4(q):
        await_bytes(m.at[q, pl.ds(0, NP - 1)], m_recv.at[q])
        v = split(m[q].reshape(NC * rows, NY * NZ * SUB))
        acc = dot3(v, (ah[...], al[...]), ((0,), (0,)))
        yo[q] = acc.reshape(yo.shape[1:])
        for j in range(1, NY):
            send(
                yo.at[q, lax.rem(y + j, NY)],
                yr.at[q, j - 1],
                yr_send.at[q],
                yr_recv.at[q],
                along_y(j),
            )

    def s5(q):
        await_bytes(yr.at[q], yr_recv.at[q])
        acc = yo[q, y]
        for j in range(NY - 1):
            acc = acc + yr[q, j]
        rz[q] = acc
        owner, i = q // per, q % per
        for d in (2, 1, 3):
            send(
                rz.at[q, d],
                zr.at[i, c * NZ + d],
                zr_send.at[q],
                zr_recv.at[i],
                along_z(d, owner),
            )

        @pl.when(c == owner)
        def _():
            zr[i, c * NZ] = acc[0]

        @pl.when(c != owner)
        def _():
            send(rz.at[q, 0], zr.at[i, c * NZ], zp_send.at[i], zr_recv.at[i], partner)

    a_own.wait()
    await_bytes(a.at[my_rows], a_recv)
    hi, lo = split(a[...])
    ah[...] = hi
    al[...] = lo
    for stage, q in STEPS:
        (forward, s1, s2, s3, s4, s5)[stage](q)

    for i in range(per):
        await_bytes(zr.at[i, pl.ds(0, NC * NZ - 1)], zr_recv.at[i])
        for k in range(NC):
            acc = zr[i, k * NZ]
            for d in range(1, NZ):
                acc = acc + zr[i, k * NZ + d]
            out[i * SUB : (i + 1) * SUB, k * half : (k + 1) * half] = acc

    await_bytes(a.at[my_rows], a_send)
    await_bytes(g.at[my_chunks, y, 0], wp_send)
    await_bytes(g.at[0, pl.ds(0, NY - 1)], go_send)
    for i in range(per):
        await_bytes(rz.at[0, 0], zp_send.at[i])
    for q in range(chunks):
        await_bytes(g.at[q, y, pl.ds(1, NZ - 1)], w_send.at[q])
        await_bytes(g.at[q, pl.ds(0, NY - 1), pl.ds(0, NZ - 1)], gy_send.at[q])
        await_bytes(rs.at[q], rs_send.at[q])
        await_bytes(zx.at[q, pl.ds(0, NL - 1)], zx_send.at[q])
        await_bytes(m.at[q, pl.ds(0, NP - 1)], m_send.at[q])
        await_bytes(yr.at[q], yr_send.at[q])
        await_bytes(rz.at[q, pl.ds(1, NZ - 1)], zr_send.at[q])


def shards(calib, weight):
    rows, feats = calib.shape
    wide = weight.shape[1]
    half = feats // NC
    part = NC * rows // NP
    per = wide // SUB
    q = NC * per
    f32, bf16 = jnp.float32, jnp.bfloat16
    cols = NY * NZ * SUB
    factor = 1.0 / math.sqrt(rows * lax.axis_size("tok"))
    dma = lambda *n: pltpu.SemaphoreType.DMA(n)
    return pl.pallas_call(
        functools.partial(kernel, factor),
        out_shape=jax.ShapeDtypeStruct((wide, feats), f32),
        in_specs=[pl.BlockSpec(memory_space=pl.ANY)] * 2,
        out_specs=pl.BlockSpec(memory_space=pltpu.VMEM),
        scratch_shapes=[
            pltpu.VMEM((NC * rows, half), f32),
            pltpu.VMEM((NC * rows, half), bf16),
            pltpu.VMEM((NC * rows, half), bf16),
            pltpu.VMEM((q, NY, NZ, SUB, half), f32),
            pltpu.VMEM((q, NP, part, cols), f32),
            pltpu.VMEM((q, NP - 1, part, cols), f32),
            pltpu.VMEM((q, NL, part, cols), f32),
            pltpu.VMEM((q, NP, part, cols), f32),
            pltpu.VMEM((q, NY, NZ, SUB, half), f32),
            pltpu.VMEM((q, NY - 1, NZ, SUB, half), f32),
            pltpu.VMEM((q, NZ, SUB, half), f32),
            pltpu.VMEM((per, NC * NZ, SUB, half), f32),
            dma(2),
            *[pltpu.SemaphoreType.DMA] * 6,
            *[dma(q) for _ in range(13)],
            dma(per),
            dma(per),
        ],
        compiler_params=pltpu.CompilerParams(
            collective_id=0,
            has_side_effects=True,
        ),
        name="gram",
    )(calib, weight.T.reshape(per, SUB, feats))


def solution(mesh):
    return jax.shard_map(
        shards,
        mesh=mesh,
        in_specs=(P("tok", "feat"), P("feat", "tok")),
        out_specs=P("tok", "feat"),
        check_vma=False,
    )
```

```python
import functools
import math

import jax
import jax.numpy as jnp
from jax import lax
from jax.experimental import pallas as pl
from jax.experimental.pallas import tpu as pltpu
from jax.sharding import PartitionSpec as P

MESH = pl.DeviceIdType.MESH
NZ, NY, NC, NX, NL = 4, 4, 2, 4, 4
NB = 2
NP = NX * NB
UP, FAR, DOWN = 1, 2, 3
SUB = 8
STEPS = (
    (8, 0), (8, 1), (0, 0), (8, 2), (0, 1), (8, 3), (1, 0), (0, 2),
    (2, 0), (1, 1), (2, 1), (0, 3), (1, 2), (3, 0), (2, 2), (3, 1),
    (1, 3), (4, 0), (2, 3), (3, 2), (4, 1), (5, 0), (3, 3), (4, 2),
    (6, 0), (5, 1), (6, 1), (4, 3), (7, 0), (5, 2), (6, 2), (7, 1),
    (5, 3), (9, 0), (6, 3), (7, 2), (9, 1), (7, 3), (9, 2), (9, 3),
)


def split(v):
    hi = v.astype(jnp.bfloat16)
    return hi, (v - hi.astype(jnp.float32)).astype(jnp.bfloat16)


def dot3(a, b, dims):
    (ah, al), (bh, bl) = a, b
    f = lambda p, q: lax.dot_general(
        p, q, (dims, ((), ())), preferred_element_type=jnp.float32
    )
    return f(ah, bh) + (f(ah, bl) + f(al, bh))


def kernel(
    factor,
    calib,
    wt,
    out,
    a,
    ah,
    al,
    w2,
    g,
    p,
    rs,
    zx,
    m,
    yo,
    yp,
    y1,
    yr,
    rz,
    rl,
    zr,
    loc_sem,
    wp_send,
    wp_recv,
    ao_send,
    an_send,
    a_recv,
    wo_send,
    wo_recv,
    w_send,
    wu_recv,
    wd_recv,
    wr_send,
    wr_recv,
    gp_send,
    gp_recv,
    gy_send,
    gy_recv,
    gb_send,
    gb_recv,
    rs_send,
    rs_recv,
    zx_send,
    zx_recv,
    m_send,
    m_recv,
    yp_send,
    yp_recv,
    yr_send,
    yr_recv,
    zr_send,
    zo_send,
    rl_send,
    rl_recv,
    zr_recv,
):
    tok, feat = lax.axis_index("tok"), lax.axis_index("feat")
    zh, y, c = tok // (NY * NC), lax.rem(tok, NY * NC) // NC, lax.rem(tok, NC)
    x, zl = feat // NL, lax.rem(feat, NL)
    b, pair = lax.rem(y, NB), y // NB
    h = lax.rem(b + pair, 2)
    mate = pair * NB + 1 - b
    near = NY - 1 - y
    yc = pair * NB + c
    yt = jnp.where(h == c, y, mate)
    pm = x * NB + b
    half = calib.shape[1] // 2
    rows = calib.shape[0]
    per = wt.shape[0]
    chunks = NC * per

    def dev(zh=zh, y=y, c=c, x=x, zl=zl):
        return ((zh * NY + y) * NC + c, x * NL + zl)

    def along_z(j):
        return lax.rem(zh + j, NZ)

    def along_l(j):
        return dev(zl=lax.rem(zl + j, NL))

    def piece(j):
        t = lax.rem(pm + j, NP)
        return t, dev(x=t // NB, y=pair * NB + lax.rem(t, NB))

    partner = dev(c=1 - c)

    def send(src, dst, ssem, rsem, to):
        pltpu.make_async_remote_copy(
            src_ref=src,
            dst_ref=dst,
            send_sem=ssem,
            recv_sem=rsem,
            device_id=to,
            device_id_type=MESH,
        ).start()

    def put(src, dst, ssem, rsem, to, here):
        @pl.when(here)
        def _():
            pltpu.make_async_copy(src, dst, rsem).start()

        @pl.when(jnp.logical_not(here))
        def _():
            send(src, dst, ssem, rsem, to)

    def await_bytes(ref, sem):
        pltpu.make_async_copy(ref, ref, sem).wait()

    def half_at(k):
        return pl.ds(pl.multiple_of(k * half, 128), half)

    my_rows = pl.ds(pl.multiple_of(c * rows, 8), rows)
    my_chunks = pl.ds(c * per, per)

    w_own = pltpu.make_async_copy(wt.at[:, :, half_at(c)], w2.at[my_chunks], loc_sem)
    w_own.start()

    barrier = pltpu.get_barrier_semaphore()

    def greet(to):
        pl.semaphore_signal(barrier, inc=1, device_id=to, device_id_type=MESH)

    for j in (1, NZ - 1):
        for k in range(NC):
            greet(dev(zh=along_z(j), c=k))
            greet(dev(zh=along_z(j), y=mate, c=k))
    greet(partner)
    greet(dev(y=mate, c=1 - c))
    greet(dev(y=near))
    for j in range(1, NL):
        greet(along_l(j))
    for j in range(1, NP):
        greet(piece(j)[1])
    pl.semaphore_wait(barrier, 2 * NC * NB + 3 + (NL - 1) + (NP - 1))

    send(wt.at[:, :, half_at(1 - c)], w2.at[my_chunks], wp_send, wp_recv, partner)
    w_own.wait()
    await_bytes(w2.at[my_chunks], wp_recv)
    for q in range(chunks):
        for j, sem in (UP, wu_recv), (DOWN, wd_recv):
            send(
                w2.at[q],
                g.at[q, 0, b, NZ - j],
                w_send.at[q],
                sem.at[q],
                dev(zh=along_z(j), y=yt, c=b),
            )
    w_here = jnp.logical_and(yt == y, b == c)
    put(w2, g.at[:, 0, b, 0], wo_send, wo_recv, dev(y=yt, c=b), w_here)
    a_here = b == c
    put(calib.at[:, half_at(h)], a.at[my_rows], ao_send, a_recv, dev(c=b), a_here)
    send(
        calib.at[:, half_at(1 - h)], a.at[my_rows], an_send, a_recv, dev(y=mate, c=b)
    )

    def onward(q):
        return (UP, wu_recv, wd_recv) if q % 2 == 0 else (DOWN, wd_recv, wu_recv)

    def s8(q):
        j, sem, _ = onward(q)
        got = g.at[q, 0, c, NZ - j]
        await_bytes(got, sem.at[q])
        send(
            got,
            g.at[q, 0, c, FAR],
            wr_send.at[q],
            wr_recv.at[q],
            dev(zh=along_z(j)),
        )

    def s0(q):
        if q == 0:
            await_bytes(w2, wo_recv)
        j, _, sem = onward(q)
        await_bytes(g.at[q, 0, c, j], sem.at[q])
        await_bytes(g.at[q, 0, c, FAR], wr_recv.at[q])
        got = g.at[q, 0, c]
        send(got, g.at[q, 1, c], gy_send.at[q], gy_recv.at[q], dev(y=near))
        send(got, got, gp_send.at[q], gp_recv.at[q], partner)

    def s1(q):
        got = g.at[q, 1, c]
        await_bytes(got, gy_recv.at[q])
        send(got, got, gb_send.at[q], gb_recv.at[q], partner)

    def s2(q):
        if q == 0:
            await_bytes(a, a_recv)
            hi, lo = split(a[...])
            ah[...] = hi
            al[...] = lo
        await_bytes(g.at[q, 0, 1 - c], gp_recv.at[q])
        await_bytes(g.at[q, 1, 1 - c], gb_recv.at[q])
        w = split(g[q].reshape(NY * NZ * SUB, half))
        acc = dot3((ah[...], al[...]), w, ((1,), (1,)))
        p[q] = acc.reshape(p.shape[1:])

        def one(j, _):
            t, to = piece(j)
            send(p.at[q, t], rs.at[q, j - 1], rs_send.at[q], rs_recv.at[q], to)
            return 0

        lax.fori_loop(1, NP, one, 0)

    def s3(q):
        await_bytes(rs.at[q], rs_recv.at[q])
        acc = p[q, pm]
        for j in range(NP - 1):
            acc = acc + rs[q, j]
        zx[q, zl] = acc
        for j in range(1, NL):
            send(zx.at[q, zl], zx.at[q, zl], zx_send.at[q], zx_recv.at[q], along_l(j))

    def s4(q):
        await_bytes(zx.at[q, pl.ds(0, NL - 1)], zx_recv.at[q])
        acc = zx[q, 0]
        for j in range(1, NL):
            acc = acc + zx[q, j]
        m[q, pm] = acc * factor

        def one(j, _):
            send(m.at[q, pm], m.at[q, pm], m_send.at[q], m_recv.at[q], piece(j)[1])
            return 0

        lax.fori_loop(1, NP, one, 0)

    def s5(q):
        await_bytes(m.at[q, pl.ds(0, NP - 1)], m_recv.at[q])
        v = split(m[q].reshape(NC * rows, NY * NZ * SUB))
        acc = dot3(v, (ah[...], al[...]), ((0,), (0,)))
        yo[q] = acc.reshape(yo.shape[1:])
        send(yo.at[q, :, 1 - c], yp.at[q], yp_send.at[q], yp_recv.at[q], partner)

    def s6(q):
        await_bytes(yp.at[q], yp_recv.at[q])
        y1[q] = yo[q, 1, c] + yp[q, 1]
        send(y1.at[q], yr.at[q], yr_send.at[q], yr_recv.at[q], dev(y=near))

    def s7(q):
        await_bytes(yr.at[q], yr_recv.at[q])
        rz[q] = yo[q, 0, c] + yp[q, 0] + yr[q]
        j, _, _ = onward(q)
        send(
            rz.at[q, FAR], rl.at[q], rl_send.at[q], rl_recv.at[q], dev(zh=along_z(j))
        )
        deliver(q, NZ - j)
        put(
            rz.at[q, 0],
            zr.at[q % per, 3 * h],
            zo_send.at[q],
            zr_recv.at[q % per],
            dev(y=yc, c=q // per),
            jnp.logical_and(yc == y, c == q // per),
        )

    def deliver(q, d):
        send(
            rz.at[q, d],
            zr.at[q % per, 3 * h + (1 if d == UP else 2)],
            zr_send.at[q],
            zr_recv.at[q % per],
            dev(zh=along_z(d), y=yc, c=q // per),
        )

    def s9(q):
        j, _, _ = onward(q)
        await_bytes(rl.at[q], rl_recv.at[q])
        rz[q, j] = rz[q, j] + rl[q]
        deliver(q, j)

    for stage, q in STEPS:
        (s0, s1, s2, s3, s4, s5, s6, s7, s8, s9)[stage](q)

    for i in range(per):
        await_bytes(zr.at[i], zr_recv.at[i])
        for k in range(2):
            acc = zr[i, 3 * k]
            for d in range(1, 3):
                acc = acc + zr[i, 3 * k + d]
            out[i * SUB : (i + 1) * SUB, k * half : (k + 1) * half] = acc

    await_bytes(w2.at[my_chunks], wp_send)
    await_bytes(a.at[my_rows], an_send)

    @pl.when(jnp.logical_not(a_here))
    def _():
        await_bytes(a.at[my_rows], ao_send)

    @pl.when(jnp.logical_not(w_here))
    def _():
        await_bytes(w2, wo_send)

    for q in range(chunks):
        await_bytes(g.at[q, 0, 0, pl.ds(0, 2)], w_send.at[q])
        await_bytes(g.at[q, 0, 0, 0], wr_send.at[q])
        await_bytes(rl.at[q], rl_send.at[q])
        await_bytes(g.at[q, 0, 0], gp_send.at[q])
        await_bytes(g.at[q, 0, 0], gy_send.at[q])
        await_bytes(g.at[q, 0, 0], gb_send.at[q])
        await_bytes(rs.at[q], rs_send.at[q])
        await_bytes(zx.at[q, pl.ds(0, NL - 1)], zx_send.at[q])
        await_bytes(m.at[q, pl.ds(0, NP - 1)], m_send.at[q])
        await_bytes(yp.at[q], yp_send.at[q])
        await_bytes(yr.at[q], yr_send.at[q])
        await_bytes(rz.at[q, pl.ds(0, 2)], zr_send.at[q])

        @pl.when(jnp.logical_not(jnp.logical_and(yc == y, c == q // per)))
        def _():
            await_bytes(rz.at[q, 0], zo_send.at[q])


def shards(calib, weight):
    rows, feats = calib.shape
    wide = weight.shape[1]
    half = feats // 2
    part = NC * rows // NP
    per = wide // SUB
    q = NC * per
    f32, bf16 = jnp.float32, jnp.bfloat16
    cols = NY * NZ * SUB
    factor = 1.0 / math.sqrt(rows * lax.axis_size("tok"))
    dma = lambda *n: pltpu.SemaphoreType.DMA(n)
    return pl.pallas_call(
        functools.partial(kernel, factor),
        out_shape=jax.ShapeDtypeStruct((wide, feats), f32),
        in_specs=[pl.BlockSpec(memory_space=pl.ANY)] * 2,
        out_specs=pl.BlockSpec(memory_space=pltpu.VMEM),
        scratch_shapes=[
            pltpu.VMEM((NC * rows, half), f32),
            pltpu.VMEM((NC * rows, half), bf16),
            pltpu.VMEM((NC * rows, half), bf16),
            pltpu.VMEM((q, SUB, half), f32),
            pltpu.VMEM((q, NY // NB, NB, NZ, SUB, half), f32),
            pltpu.VMEM((q, NP, part, cols), f32),
            pltpu.VMEM((q, NP - 1, part, cols), f32),
            pltpu.VMEM((q, NL, part, cols), f32),
            pltpu.VMEM((q, NP, part, cols), f32),
            pltpu.VMEM((q, NY // NB, NB, NZ, SUB, half), f32),
            pltpu.VMEM((q, NY // NB, NZ, SUB, half), f32),
            pltpu.VMEM((q, NZ, SUB, half), f32),
            pltpu.VMEM((q, NZ, SUB, half), f32),
            pltpu.VMEM((q, NZ, SUB, half), f32),
            pltpu.VMEM((q, SUB, half), f32),
            pltpu.VMEM((per, 2 * 3, SUB, half), f32),
            *[pltpu.SemaphoreType.DMA] * 8,
            *[dma(q) for _ in range(25)],
            dma(per),
        ],
        compiler_params=pltpu.CompilerParams(collective_id=0, has_side_effects=True),
        name="gram",
    )(calib, weight.T.reshape(per, SUB, feats))


def solution(mesh):
    return jax.shard_map(
        shards,
        mesh=mesh,
        in_specs=(P("tok", "feat"), P("feat", "tok")),
        out_specs=P("tok", "feat"),
        check_vma=False,
    )
```

```python
import functools
import math

import jax
import jax.numpy as jnp
from jax import lax
from jax.experimental import pallas as pl
from jax.experimental.pallas import tpu as pltpu
from jax.sharding import PartitionSpec as P

MESH = pl.DeviceIdType.MESH
NZ, NY, NC, NX, NL = 4, 4, 2, 4, 4
NB = 2
NP = NX * NB
UP, FAR, DOWN = 1, 2, 3
SLOT = (0, 1, 3, 2)
SUB = 8
STEPS = (
    (10, 1), (10, 0), (10, 2), (10, 3), (8, 1), (8, 0), (8, 2), (8, 3),
    (0, 0), (0, 1), (1, 0), (1, 1), (0, 2), (2, 0), (0, 3), (2, 1),
    (1, 2), (1, 3), (2, 2), (3, 0), (2, 3), (3, 1), (3, 2), (4, 0),
    (3, 3), (4, 1), (4, 2), (5, 0), (4, 3), (5, 1), (6, 0), (6, 1),
    (5, 2), (5, 3), (7, 0), (6, 2), (7, 1), (6, 3), (7, 2), (7, 3),
    (9, 1), (9, 0), (9, 2), (9, 3),
)


def first(stage):
    return next(q for s, q in STEPS if s == stage)


LEAD = sum(1 for k, s in enumerate(STEPS) if all(t[0] == 10 for t in STEPS[: k + 1]))


def split(v):
    hi = v.astype(jnp.bfloat16)
    return hi, (v - hi.astype(jnp.float32)).astype(jnp.bfloat16)


def dot3(a, b, dims):
    (ah, al), (bh, bl) = a, b
    f = lambda p, q: lax.dot_general(
        p, q, (dims, ((), ())), preferred_element_type=jnp.float32
    )
    return f(ah, bh) + (f(ah, bl) + f(al, bh))


def kernel(
    factor,
    calib,
    wt,
    out,
    a,
    ah,
    al,
    w2,
    g,
    p,
    rs,
    zx,
    m,
    yo,
    yp,
    y1,
    yr,
    rz,
    rl,
    zr,
    loc_sem,
    wp_send,
    wp_recv,
    ao_send,
    an_send,
    a_recv,
    wo_send,
    wo_recv,
    w_send,
    wu_recv,
    wd_recv,
    wr_send,
    wr_recv,
    gp_send,
    gp_recv,
    gy_send,
    gy_recv,
    gb_send,
    gb_recv,
    rs_send,
    rs_recv,
    zx_send,
    zx_recv,
    m_send,
    m_recv,
    yp_send,
    yp_recv,
    yr_send,
    yr_recv,
    zr_send,
    zo_send,
    rl_send,
    rl_recv,
    zr_recv,
):
    tok, feat = lax.axis_index("tok"), lax.axis_index("feat")
    zh, y, c = tok // (NY * NC), lax.rem(tok, NY * NC) // NC, lax.rem(tok, NC)
    x, zl = feat // NL, lax.rem(feat, NL)
    b, pair = lax.rem(y, NB), y // NB
    h = lax.rem(b + pair, 2)
    mate = pair * NB + 1 - b
    near = NY - 1 - y
    yc = pair * NB + c
    yt = jnp.where(h == c, y, mate)
    pm = x * NB + b
    half = calib.shape[1] // 2
    rows = calib.shape[0]
    per = wt.shape[0]
    chunks = NC * per

    def dev(zh=zh, y=y, c=c, x=x, zl=zl):
        return ((zh * NY + y) * NC + c, x * NL + zl)

    def along_z(j):
        return lax.rem(zh + j, NZ)

    def along_l(j):
        return dev(zl=lax.rem(zl + j, NL))

    def piece(j):
        t = lax.rem(pm + j, NP)
        return t, dev(x=t // NB, y=pair * NB + lax.rem(t, NB))

    partner = dev(c=1 - c)

    def send(src, dst, ssem, rsem, to):
        pltpu.make_async_remote_copy(
            src_ref=src,
            dst_ref=dst,
            send_sem=ssem,
            recv_sem=rsem,
            device_id=to,
            device_id_type=MESH,
        ).start()

    def put(src, dst, ssem, rsem, to, here):
        @pl.when(here)
        def _():
            pltpu.make_async_copy(src, dst, rsem).start()

        @pl.when(jnp.logical_not(here))
        def _():
            send(src, dst, ssem, rsem, to)

    def await_bytes(ref, sem):
        pltpu.make_async_copy(ref, ref, sem).wait()

    def half_at(k):
        return pl.ds(pl.multiple_of(k * half, 128), half)

    my_rows = pl.ds(pl.multiple_of(c * rows, 8), rows)
    my_chunks = pl.ds(c * per, per)

    w_own = pltpu.make_async_copy(wt.at[:, :, half_at(c)], w2.at[my_chunks], loc_sem)
    w_own.start()

    barrier = pltpu.get_barrier_semaphore()

    def greet(to):
        pl.semaphore_signal(barrier, inc=1, device_id=to, device_id_type=MESH)

    for j in (1, NZ - 1):
        for k in range(NC):
            greet(dev(zh=along_z(j), c=k))
            greet(dev(zh=along_z(j), y=mate, c=k))
    greet(partner)
    greet(dev(y=mate, c=1 - c))
    greet(dev(y=near))
    for j in range(1, NL):
        greet(along_l(j))
    for j in range(1, NP):
        greet(piece(j)[1])
    pl.semaphore_wait(barrier, 2 * NC * NB + 3 + (NL - 1) + (NP - 1))

    send(wt.at[:, :, half_at(1 - c)], w2.at[my_chunks], wp_send, wp_recv, partner)
    w_own.wait()
    await_bytes(w2.at[my_chunks], wp_recv)
    def s10(q):
        for j, sem in (UP, wu_recv), (DOWN, wd_recv):
            send(
                w2.at[q],
                g.at[q, 0, b, SLOT[NZ - j]],
                w_send.at[q],
                sem.at[q],
                dev(zh=along_z(j), y=yt, c=b),
            )

    for stage, q in STEPS[:LEAD]:
        s10(q)
    w_here = jnp.logical_and(yt == y, b == c)
    put(w2, g.at[:, 0, b, 0], wo_send, wo_recv, dev(y=yt, c=b), w_here)
    a_here = b == c
    put(calib.at[:, half_at(h)], a.at[my_rows], ao_send, a_recv, dev(c=b), a_here)
    send(
        calib.at[:, half_at(1 - h)], a.at[my_rows], an_send, a_recv, dev(y=mate, c=b)
    )

    def onward(q):
        return (UP, wu_recv, wd_recv) if q % 2 == 0 else (DOWN, wd_recv, wu_recv)

    def share(q, got):
        dst = g.at[q, 1, c, got]
        got = g.at[q, 0, c, got]
        send(got, dst, gy_send.at[q], gy_recv.at[q], dev(y=near))
        send(got, got, gp_send.at[q], gp_recv.at[q], partner)

    def s8(q):
        j, sem, other = onward(q)
        got = g.at[q, 0, c, SLOT[NZ - j]]
        await_bytes(got, sem.at[q])
        send(
            got,
            g.at[q, 0, c, SLOT[FAR]],
            wr_send.at[q],
            wr_recv.at[q],
            dev(zh=along_z(j)),
        )
        if q == first(8):
            await_bytes(w2, wo_recv)
        await_bytes(g.at[q, 0, c, SLOT[j]], other.at[q])
        share(q, pl.ds(0, NZ - 1))

    def s0(q):
        await_bytes(g.at[q, 0, c, SLOT[FAR]], wr_recv.at[q])
        share(q, pl.ds(NZ - 1, 1))

    def s1(q):
        got = g.at[q, 1, c]
        await_bytes(got, gy_recv.at[q])
        send(got, got, gb_send.at[q], gb_recv.at[q], partner)

    def s2(q):
        if q == first(2):
            await_bytes(a, a_recv)
            hi, lo = split(a[...])
            ah[...] = hi
            al[...] = lo
        await_bytes(g.at[q, 0, 1 - c], gp_recv.at[q])
        await_bytes(g.at[q, 1, 1 - c], gb_recv.at[q])
        w = split(g[q].reshape(NY * NZ * SUB, half))
        acc = dot3((ah[...], al[...]), w, ((1,), (1,)))
        p[q] = acc.reshape(p.shape[1:])

        def one(j, _):
            t, to = piece(j)
            send(p.at[q, t], rs.at[q, j - 1], rs_send.at[q], rs_recv.at[q], to)
            return 0

        lax.fori_loop(1, NP, one, 0)

    def s3(q):
        await_bytes(rs.at[q], rs_recv.at[q])
        acc = p[q, pm]
        for j in range(NP - 1):
            acc = acc + rs[q, j]
        zx[q, zl] = acc
        for j in range(1, NL):
            send(zx.at[q, zl], zx.at[q, zl], zx_send.at[q], zx_recv.at[q], along_l(j))

    def s4(q):
        await_bytes(zx.at[q, pl.ds(0, NL - 1)], zx_recv.at[q])
        acc = zx[q, 0]
        for j in range(1, NL):
            acc = acc + zx[q, j]
        m[q, pm] = acc * factor

        def one(j, _):
            send(m.at[q, pm], m.at[q, pm], m_send.at[q], m_recv.at[q], piece(j)[1])
            return 0

        lax.fori_loop(1, NP, one, 0)

    def s5(q):
        await_bytes(m.at[q, pl.ds(0, NP - 1)], m_recv.at[q])
        v = split(m[q].reshape(NC * rows, NY * NZ * SUB))
        acc = dot3(v, (ah[...], al[...]), ((0,), (0,)))
        yo[q] = acc.reshape(yo.shape[1:])
        send(yo.at[q, :, 1 - c], yp.at[q], yp_send.at[q], yp_recv.at[q], partner)

    def s6(q):
        await_bytes(yp.at[q], yp_recv.at[q])
        y1[q] = yo[q, 1, c] + yp[q, 1]
        send(y1.at[q], yr.at[q], yr_send.at[q], yr_recv.at[q], dev(y=near))

    def s7(q):
        await_bytes(yr.at[q], yr_recv.at[q])
        rz[q] = yo[q, 0, c] + yp[q, 0] + yr[q]
        j, _, _ = onward(q)
        send(
            rz.at[q, SLOT[FAR]], rl.at[q], rl_send.at[q], rl_recv.at[q], dev(zh=along_z(j))
        )
        deliver(q, NZ - j)
        put(
            rz.at[q, 0],
            zr.at[q % per, 3 * h],
            zo_send.at[q],
            zr_recv.at[q % per],
            dev(y=yc, c=q // per),
            jnp.logical_and(yc == y, c == q // per),
        )

    def deliver(q, d):
        send(
            rz.at[q, SLOT[d]],
            zr.at[q % per, 3 * h + SLOT[d]],
            zr_send.at[q],
            zr_recv.at[q % per],
            dev(zh=along_z(d), y=yc, c=q // per),
        )

    def s9(q):
        j, _, _ = onward(q)
        await_bytes(rl.at[q], rl_recv.at[q])
        rz[q, SLOT[j]] = rz[q, SLOT[j]] + rl[q]
        deliver(q, j)

    for stage, q in STEPS[LEAD:]:
        (s0, s1, s2, s3, s4, s5, s6, s7, s8, s9, s10)[stage](q)

    for i in range(per):
        await_bytes(zr.at[i], zr_recv.at[i])
        for k in range(2):
            acc = zr[i, 3 * k]
            for d in range(1, 3):
                acc = acc + zr[i, 3 * k + d]
            out[i * SUB : (i + 1) * SUB, k * half : (k + 1) * half] = acc

    await_bytes(w2.at[my_chunks], wp_send)
    await_bytes(a.at[my_rows], an_send)

    @pl.when(jnp.logical_not(a_here))
    def _():
        await_bytes(a.at[my_rows], ao_send)

    @pl.when(jnp.logical_not(w_here))
    def _():
        await_bytes(w2, wo_send)

    for q in range(chunks):
        await_bytes(g.at[q, 0, 0, pl.ds(0, 2)], w_send.at[q])
        await_bytes(g.at[q, 0, 0, 0], wr_send.at[q])
        await_bytes(rl.at[q], rl_send.at[q])
        await_bytes(g.at[q, 0, 0], gp_send.at[q])
        await_bytes(g.at[q, 0, 0], gy_send.at[q])
        await_bytes(g.at[q, 0, 0], gb_send.at[q])
        await_bytes(rs.at[q], rs_send.at[q])
        await_bytes(zx.at[q, pl.ds(0, NL - 1)], zx_send.at[q])
        await_bytes(m.at[q, pl.ds(0, NP - 1)], m_send.at[q])
        await_bytes(yp.at[q], yp_send.at[q])
        await_bytes(yr.at[q], yr_send.at[q])
        await_bytes(rz.at[q, pl.ds(0, 2)], zr_send.at[q])

        @pl.when(jnp.logical_not(jnp.logical_and(yc == y, c == q // per)))
        def _():
            await_bytes(rz.at[q, 0], zo_send.at[q])


def shards(calib, weight):
    rows, feats = calib.shape
    wide = weight.shape[1]
    half = feats // 2
    part = NC * rows // NP
    per = wide // SUB
    q = NC * per
    f32, bf16 = jnp.float32, jnp.bfloat16
    cols = NY * NZ * SUB
    factor = 1.0 / math.sqrt(rows * lax.axis_size("tok"))
    dma = lambda *n: pltpu.SemaphoreType.DMA(n)
    return pl.pallas_call(
        functools.partial(kernel, factor),
        out_shape=jax.ShapeDtypeStruct((wide, feats), f32),
        in_specs=[pl.BlockSpec(memory_space=pl.ANY)] * 2,
        out_specs=pl.BlockSpec(memory_space=pltpu.VMEM),
        scratch_shapes=[
            pltpu.VMEM((NC * rows, half), f32),
            pltpu.VMEM((NC * rows, half), bf16),
            pltpu.VMEM((NC * rows, half), bf16),
            pltpu.VMEM((q, SUB, half), f32),
            pltpu.VMEM((q, NY // NB, NB, NZ, SUB, half), f32),
            pltpu.VMEM((q, NP, part, cols), f32),
            pltpu.VMEM((q, NP - 1, part, cols), f32),
            pltpu.VMEM((q, NL, part, cols), f32),
            pltpu.VMEM((q, NP, part, cols), f32),
            pltpu.VMEM((q, NY // NB, NB, NZ, SUB, half), f32),
            pltpu.VMEM((q, NY // NB, NZ, SUB, half), f32),
            pltpu.VMEM((q, NZ, SUB, half), f32),
            pltpu.VMEM((q, NZ, SUB, half), f32),
            pltpu.VMEM((q, NZ, SUB, half), f32),
            pltpu.VMEM((q, SUB, half), f32),
            pltpu.VMEM((per, 2 * 3, SUB, half), f32),
            *[pltpu.SemaphoreType.DMA] * 8,
            *[dma(q) for _ in range(25)],
            dma(per),
        ],
        compiler_params=pltpu.CompilerParams(collective_id=0, has_side_effects=True),
        name="gram",
    )(calib, weight.T.reshape(per, SUB, feats))


def solution(mesh):
    return jax.shard_map(
        shards,
        mesh=mesh,
        in_specs=(P("tok", "feat"), P("feat", "tok")),
        out_specs=P("tok", "feat"),
        check_vma=False,
    )
```

```python
import functools
import math

import jax
import jax.numpy as jnp
from jax import lax
from jax.experimental import pallas as pl
from jax.experimental.pallas import tpu as pltpu
from jax.sharding import PartitionSpec as P

MESH = pl.DeviceIdType.MESH
NZ, NY, NC, NX, NL = 4, 4, 2, 4, 4
NB = 2
NP = NX * NB
UP, FAR, DOWN = 1, 2, 3
FARTHEST = (4, 3, 5, 2, 6, 1, 7)
SLOT = (0, 1, 3, 2)
SUB = 8
STEPS = (
    (10, 0), (10, 1), (10, 2), (10, 3), (8, 0), (8, 1), (0, 0), (8, 2),
    (8, 3), (0, 1), (1, 0), (2, 0), (0, 2), (1, 1), (2, 1), (0, 3),
    (1, 2), (2, 2), (3, 0), (1, 3), (2, 3), (3, 1), (4, 0), (3, 2),
    (4, 1), (5, 0), (3, 3), (4, 2), (6, 0), (5, 1), (4, 3), (6, 1),
    (5, 2), (6, 2), (7, 0), (5, 3), (6, 3), (7, 1), (9, 0), (7, 2),
    (7, 3), (9, 1), (9, 2), (9, 3),
)


def first(stage):
    return next(q for s, q in STEPS if s == stage)


LEAD = sum(1 for k, s in enumerate(STEPS) if all(t[0] == 10 for t in STEPS[: k + 1]))


def split(v):
    hi = v.astype(jnp.bfloat16)
    return hi, (v - hi.astype(jnp.float32)).astype(jnp.bfloat16)


def dot3(a, b, dims):
    (ah, al), (bh, bl) = a, b
    f = lambda p, q: lax.dot_general(
        p, q, (dims, ((), ())), preferred_element_type=jnp.float32
    )
    return f(ah, bh) + (f(ah, bl) + f(al, bh))


def kernel(
    factor,
    calib,
    wt,
    out,
    a,
    ah,
    al,
    w2,
    g,
    p,
    rs,
    zx,
    m,
    yo,
    yp,
    y1,
    yr,
    rz,
    rl,
    zr,
    loc_sem,
    wp_send,
    wp_recv,
    ao_send,
    an_send,
    a_recv,
    wo_send,
    wo_recv,
    w_send,
    wu_recv,
    wd_recv,
    wr_send,
    wr_recv,
    gp_send,
    gp_recv,
    gy_send,
    gy_recv,
    gb_send,
    gb_recv,
    rs_send,
    rs_recv,
    zx_send,
    zx_recv,
    m_send,
    m_recv,
    yp_send,
    yp_recv,
    yr_send,
    yr_recv,
    zr_send,
    zo_send,
    rl_send,
    rl_recv,
    zr_recv,
):
    tok, feat = lax.axis_index("tok"), lax.axis_index("feat")
    zh, y, c = tok // (NY * NC), lax.rem(tok, NY * NC) // NC, lax.rem(tok, NC)
    x, zl = feat // NL, lax.rem(feat, NL)
    b, pair = lax.rem(y, NB), y // NB
    h = lax.rem(b + pair, 2)
    mate = pair * NB + 1 - b
    near = NY - 1 - y
    yc = pair * NB + c
    yt = jnp.where(h == c, y, mate)
    pm = x * NB + b
    half = calib.shape[1] // 2
    rows = calib.shape[0]
    cut = half // 256 * 128 + 128
    per = wt.shape[0]
    chunks = NC * per

    def dev(zh=zh, y=y, c=c, x=x, zl=zl):
        return ((zh * NY + y) * NC + c, x * NL + zl)

    def along_z(j):
        return lax.rem(zh + j, NZ)

    def along_l(j):
        return dev(zl=lax.rem(zl + j, NL))

    def piece(j):
        t = lax.rem(pm + j, NP)
        return t, dev(x=t // NB, y=pair * NB + lax.rem(t, NB))

    partner = dev(c=1 - c)

    def send(src, dst, ssem, rsem, to):
        pltpu.make_async_remote_copy(
            src_ref=src,
            dst_ref=dst,
            send_sem=ssem,
            recv_sem=rsem,
            device_id=to,
            device_id_type=MESH,
        ).start()

    def put(src, dst, ssem, rsem, to, here):
        @pl.when(here)
        def _():
            pltpu.make_async_copy(src, dst, rsem).start()

        @pl.when(jnp.logical_not(here))
        def _():
            send(src, dst, ssem, rsem, to)

    def await_bytes(ref, sem):
        pltpu.make_async_copy(ref, ref, sem).wait()

    def half_at(k):
        return pl.ds(pl.multiple_of(k * half, 128), half)

    my_rows = pl.ds(pl.multiple_of(c * rows, 8), rows)
    my_chunks = pl.ds(c * per, per)

    w_own = pltpu.make_async_copy(wt.at[:, :, half_at(c)], w2.at[my_chunks], loc_sem)
    w_own.start()

    barrier = pltpu.get_barrier_semaphore()

    def greet(to):
        pl.semaphore_signal(barrier, inc=1, device_id=to, device_id_type=MESH)

    for j in (1, NZ - 1):
        for k in range(NC):
            greet(dev(zh=along_z(j), c=k))
            greet(dev(zh=along_z(j), y=mate, c=k))
    greet(partner)
    greet(dev(y=mate, c=1 - c))
    greet(dev(y=near))
    for j in range(1, NL):
        greet(along_l(j))
    for j in range(1, NP):
        greet(piece(j)[1])
    pl.semaphore_wait(barrier, 2 * NC * NB + 3 + (NL - 1) + (NP - 1))

    send(wt.at[:, :, half_at(1 - c)], w2.at[my_chunks], wp_send, wp_recv, partner)
    w_own.wait()
    await_bytes(w2.at[my_chunks], wp_recv)
    def s10(q):
        for j, sem in (UP, wu_recv), (DOWN, wd_recv):
            send(
                w2.at[q],
                g.at[q, 0, b, SLOT[NZ - j]],
                w_send.at[q],
                sem.at[q],
                dev(zh=along_z(j), y=yt, c=b),
            )

    for stage, q in STEPS[:LEAD]:
        s10(q)
    w_here = jnp.logical_and(yt == y, b == c)
    put(w2, g.at[:, 0, b, 0], wo_send, wo_recv, dev(y=yt, c=b), w_here)
    a_here = b == c
    put(calib.at[:, half_at(h)], a.at[my_rows], ao_send, a_recv, dev(c=b), a_here)
    send(
        calib.at[:, half_at(1 - h)], a.at[my_rows], an_send, a_recv, dev(y=mate, c=b)
    )

    ways = ((UP, pl.ds(0, cut)), (DOWN, pl.ds(cut, half - cut)))

    def share(q, got):
        dst = g.at[q, 1, c, got]
        got = g.at[q, 0, c, got]
        send(got, dst, gy_send.at[q], gy_recv.at[q], dev(y=near))
        send(got, got, gp_send.at[q], gp_recv.at[q], partner)

    def s8(q):
        for (j, lanes), sem in zip(ways, (wu_recv, wd_recv)):
            got = g.at[q, 0, c, SLOT[NZ - j]]
            await_bytes(got, sem.at[q])
            send(
                got.at[:, lanes],
                g.at[q, 0, c, SLOT[FAR], :, lanes],
                wr_send.at[q],
                wr_recv.at[q],
                dev(zh=along_z(j)),
            )
        if q == first(8):
            await_bytes(w2, wo_recv)
        share(q, pl.ds(0, NZ - 1))

    def s0(q):
        await_bytes(g.at[q, 0, c, SLOT[FAR]], wr_recv.at[q])
        share(q, pl.ds(NZ - 1, 1))

    def s1(q):
        got = g.at[q, 1, c]
        await_bytes(got, gy_recv.at[q])
        send(got, got, gb_send.at[q], gb_recv.at[q], partner)

    def s2(q):
        if q == first(2):
            await_bytes(a, a_recv)
            hi, lo = split(a[...])
            ah[...] = hi
            al[...] = lo
        await_bytes(g.at[q, 0, 1 - c], gp_recv.at[q])
        await_bytes(g.at[q, 1, 1 - c], gb_recv.at[q])
        w = split(g[q].reshape(NY * NZ * SUB, half))
        acc = dot3((ah[...], al[...]), w, ((1,), (1,)))
        p[q] = acc.reshape(p.shape[1:])

        for j in FARTHEST:
            t, to = piece(j)
            send(p.at[q, t], rs.at[q, j - 1], rs_send.at[q], rs_recv.at[q], to)

    def s3(q):
        await_bytes(rs.at[q], rs_recv.at[q])
        acc = p[q, pm]
        for j in range(NP - 1):
            acc = acc + rs[q, j]
        zx[q, zl] = acc
        for j in range(1, NL):
            send(zx.at[q, zl], zx.at[q, zl], zx_send.at[q], zx_recv.at[q], along_l(j))

    def s4(q):
        await_bytes(zx.at[q, pl.ds(0, NL - 1)], zx_recv.at[q])
        acc = zx[q, 0]
        for j in range(1, NL):
            acc = acc + zx[q, j]
        m[q, pm] = acc * factor

        for j in FARTHEST:
            send(m.at[q, pm], m.at[q, pm], m_send.at[q], m_recv.at[q], piece(j)[1])

    def s5(q):
        await_bytes(m.at[q, pl.ds(0, NP - 1)], m_recv.at[q])
        v = split(m[q].reshape(NC * rows, NY * NZ * SUB))
        acc = dot3(v, (ah[...], al[...]), ((0,), (0,)))
        yo[q] = acc.reshape(yo.shape[1:])
        send(yo.at[q, :, 1 - c], yp.at[q], yp_send.at[q], yp_recv.at[q], partner)

    def s6(q):
        await_bytes(yp.at[q], yp_recv.at[q])
        y1[q] = yo[q, 1, c] + yp[q, 1]
        send(y1.at[q], yr.at[q], yr_send.at[q], yr_recv.at[q], dev(y=near))

    def s7(q):
        await_bytes(yr.at[q], yr_recv.at[q])
        rz[q] = yo[q, 0, c] + yp[q, 0] + yr[q]
        for j, lanes in ways:
            send(
                rz.at[q, SLOT[FAR], :, lanes],
                rl.at[q, :, lanes],
                rl_send.at[q],
                rl_recv.at[q],
                dev(zh=along_z(j)),
            )
        for j, lanes in ways:
            deliver(q, NZ - j, lanes)
        put(
            rz.at[q, 0],
            zr.at[q % per, 3 * h],
            zo_send.at[q],
            zr_recv.at[q % per],
            dev(y=yc, c=q // per),
            jnp.logical_and(yc == y, c == q // per),
        )

    def deliver(q, d, lanes):
        send(
            rz.at[q, SLOT[d], :, lanes],
            zr.at[q % per, 3 * h + SLOT[d], :, lanes],
            zr_send.at[q],
            zr_recv.at[q % per],
            dev(zh=along_z(d), y=yc, c=q // per),
        )

    def s9(q):
        await_bytes(rl.at[q], rl_recv.at[q])
        for j, lanes in ways:
            rz[q, SLOT[j], :, lanes] = rz[q, SLOT[j], :, lanes] + rl[q, :, lanes]
            deliver(q, j, lanes)

    for stage, q in STEPS[LEAD:]:
        (s0, s1, s2, s3, s4, s5, s6, s7, s8, s9, s10)[stage](q)

    for i in range(per):
        await_bytes(zr.at[i], zr_recv.at[i])
        for k in range(2):
            acc = zr[i, 3 * k]
            for d in range(1, 3):
                acc = acc + zr[i, 3 * k + d]
            out[i * SUB : (i + 1) * SUB, k * half : (k + 1) * half] = acc

    await_bytes(w2.at[my_chunks], wp_send)
    await_bytes(a.at[my_rows], an_send)

    @pl.when(jnp.logical_not(a_here))
    def _():
        await_bytes(a.at[my_rows], ao_send)

    @pl.when(jnp.logical_not(w_here))
    def _():
        await_bytes(w2, wo_send)

    for q in range(chunks):
        await_bytes(g.at[q, 0, 0, pl.ds(0, 2)], w_send.at[q])
        await_bytes(g.at[q, 0, 0, 0], wr_send.at[q])
        await_bytes(rl.at[q], rl_send.at[q])
        await_bytes(g.at[q, 0, 0], gp_send.at[q])
        await_bytes(g.at[q, 0, 0], gy_send.at[q])
        await_bytes(g.at[q, 0, 0], gb_send.at[q])
        await_bytes(rs.at[q], rs_send.at[q])
        await_bytes(zx.at[q, pl.ds(0, NL - 1)], zx_send.at[q])
        await_bytes(m.at[q, pl.ds(0, NP - 1)], m_send.at[q])
        await_bytes(yp.at[q], yp_send.at[q])
        await_bytes(yr.at[q], yr_send.at[q])
        await_bytes(rz.at[q, pl.ds(0, 2)], zr_send.at[q])

        @pl.when(jnp.logical_not(jnp.logical_and(yc == y, c == q // per)))
        def _():
            await_bytes(rz.at[q, 0], zo_send.at[q])


def shards(calib, weight):
    rows, feats = calib.shape
    wide = weight.shape[1]
    half = feats // 2
    part = NC * rows // NP
    per = wide // SUB
    q = NC * per
    f32, bf16 = jnp.float32, jnp.bfloat16
    cols = NY * NZ * SUB
    factor = 1.0 / math.sqrt(rows * lax.axis_size("tok"))
    in_hbm = lambda v: pltpu.with_memory_space_constraint(v, pltpu.HBM)
    dma = lambda *n: pltpu.SemaphoreType.DMA(n)
    return pl.pallas_call(
        functools.partial(kernel, factor),
        out_shape=jax.ShapeDtypeStruct((wide, feats), f32),
        in_specs=[pl.BlockSpec(memory_space=pl.ANY)] * 2,
        out_specs=pl.BlockSpec(memory_space=pltpu.VMEM),
        scratch_shapes=[
            pltpu.VMEM((NC * rows, half), f32),
            pltpu.VMEM((NC * rows, half), bf16),
            pltpu.VMEM((NC * rows, half), bf16),
            pltpu.VMEM((q, SUB, half), f32),
            pltpu.VMEM((q, NY // NB, NB, NZ, SUB, half), f32),
            pltpu.VMEM((q, NP, part, cols), f32),
            pltpu.VMEM((q, NP - 1, part, cols), f32),
            pltpu.VMEM((q, NL, part, cols), f32),
            pltpu.VMEM((q, NP, part, cols), f32),
            pltpu.VMEM((q, NY // NB, NB, NZ, SUB, half), f32),
            pltpu.VMEM((q, NY // NB, NZ, SUB, half), f32),
            pltpu.VMEM((q, NZ, SUB, half), f32),
            pltpu.VMEM((q, NZ, SUB, half), f32),
            pltpu.VMEM((q, NZ, SUB, half), f32),
            pltpu.VMEM((q, SUB, half), f32),
            pltpu.VMEM((per, 2 * 3, SUB, half), f32),
            *[pltpu.SemaphoreType.DMA] * 8,
            *[dma(q) for _ in range(25)],
            dma(per),
        ],
        compiler_params=pltpu.CompilerParams(
            collective_id=0, has_side_effects=True, vmem_limit_bytes=48 * 1024 * 1024
        ),
        name="gram",
    )(in_hbm(calib), in_hbm(weight.T.reshape(per, SUB, feats)))


def solution(mesh):
    return jax.shard_map(
        shards,
        mesh=mesh,
        in_specs=(P("tok", "feat"), P("feat", "tok")),
        out_specs=P("tok", "feat"),
        check_vma=False,
    )
```

```python
import functools
import math

import jax
import jax.numpy as jnp
from jax import lax
from jax.experimental import pallas as pl
from jax.experimental.pallas import tpu as pltpu
from jax.sharding import PartitionSpec as P

MESH = pl.DeviceIdType.MESH
NZ, NY, NC, NX, NL = 4, 4, 2, 4, 4
NB = 2
NP = NX * NB
UP, FAR, DOWN = 1, 2, 3
FARTHEST = (1, 7, 2, 6, 3, 5, 4)
SLOT = (0, 1, 3, 2)
SUB = 8
STEPS = (
    (10, 0), (10, 1), (10, 2), (10, 3), (8, 0), (8, 1), (1, 0), (8, 2),
    (0, 0), (8, 3), (1, 1), (0, 1), (2, 0), (1, 2), (0, 2), (2, 1),
    (1, 3), (0, 3), (2, 2), (3, 0), (2, 3), (3, 1), (4, 0), (3, 2),
    (4, 1), (5, 0), (3, 3), (4, 2), (6, 0), (5, 1), (4, 3), (6, 1),
    (5, 2), (6, 2), (7, 0), (5, 3), (6, 3), (7, 1), (9, 0), (7, 2),
    (7, 3), (9, 1), (9, 2), (9, 3),
)


def first(stage):
    return next(q for s, q in STEPS if s == stage)


LEAD = sum(1 for k, s in enumerate(STEPS) if all(t[0] == 10 for t in STEPS[: k + 1]))


def split(v):
    hi = v.astype(jnp.bfloat16)
    return hi, (v - hi.astype(jnp.float32)).astype(jnp.bfloat16)


def dot3(a, b, dims):
    (ah, al), (bh, bl) = a, b
    f = lambda p, q: lax.dot_general(
        p, q, (dims, ((), ())), preferred_element_type=jnp.float32
    )
    return f(ah, bh) + (f(ah, bl) + f(al, bh))


def kernel(
    factor,
    calib,
    wt,
    out,
    a,
    ah,
    al,
    w2,
    g,
    p,
    rs,
    zx,
    m,
    yo,
    yp,
    y1,
    yr,
    rz,
    rl,
    zr,
    loc_sem,
    wp_send,
    wp_recv,
    ao_send,
    an_send,
    a_recv,
    wo_send,
    wo_recv,
    w_send,
    wu_recv,
    wd_recv,
    wr_send,
    wr_recv,
    gp_send,
    gp_recv,
    gy_send,
    gy_recv,
    gb_send,
    gb_recv,
    gf_send,
    gf_recv,
    rs_send,
    rs_recv,
    zx_send,
    zx_recv,
    m_send,
    m_recv,
    yp_send,
    yp_recv,
    yr_send,
    yr_recv,
    zr_send,
    zo_send,
    rl_send,
    rl_recv,
    zr_recv,
):
    tok, feat = lax.axis_index("tok"), lax.axis_index("feat")
    zh, y, c = tok // (NY * NC), lax.rem(tok, NY * NC) // NC, lax.rem(tok, NC)
    x, zl = feat // NL, lax.rem(feat, NL)
    b, pair = lax.rem(y, NB), y // NB
    h = lax.rem(b + pair, 2)
    mate = pair * NB + 1 - b
    near = NY - 1 - y
    yc = pair * NB + c
    yt = jnp.where(h == c, y, mate)
    pm = x * NB + b
    half = calib.shape[1] // 2
    rows = calib.shape[0]
    cut = half // 256 * 128 + 128
    per = wt.shape[0]
    chunks = NC * per

    def dev(zh=zh, y=y, c=c, x=x, zl=zl):
        return ((zh * NY + y) * NC + c, x * NL + zl)

    def along_z(j):
        return lax.rem(zh + j, NZ)

    def along_l(j):
        low = zl < NL // 2
        to = (
            jnp.where(low, 1 - zl, 2 * NL - 3 - zl),
            jnp.where(low, NL - 2, 1),
            jnp.where(low, NL - 1, 0),
        )
        return dev(zl=to[j - 1])

    def piece(j):
        t = lax.rem(pm + j, NP)
        return t, dev(x=t // NB, y=pair * NB + lax.rem(t, NB))

    partner = dev(c=1 - c)

    def send(src, dst, ssem, rsem, to):
        pltpu.make_async_remote_copy(
            src_ref=src,
            dst_ref=dst,
            send_sem=ssem,
            recv_sem=rsem,
            device_id=to,
            device_id_type=MESH,
        ).start()

    def put(src, dst, ssem, rsem, to, here):
        @pl.when(here)
        def _():
            pltpu.make_async_copy(src, dst, rsem).start()

        @pl.when(jnp.logical_not(here))
        def _():
            send(src, dst, ssem, rsem, to)

    def await_bytes(ref, sem):
        pltpu.make_async_copy(ref, ref, sem).wait()

    def half_at(k):
        return pl.ds(pl.multiple_of(k * half, 128), half)

    my_rows = pl.ds(pl.multiple_of(c * rows, 8), rows)
    my_chunks = pl.ds(c * per, per)
    most = pl.ds(0, NZ - 1)

    w_own = pltpu.make_async_copy(wt.at[:, :, half_at(c)], w2.at[my_chunks], loc_sem)
    w_own.start()

    barrier = pltpu.get_barrier_semaphore()

    def greet(to):
        pl.semaphore_signal(barrier, inc=1, device_id=to, device_id_type=MESH)

    for j in (1, NZ - 1):
        for k in range(NC):
            greet(dev(zh=along_z(j), c=k))
            greet(dev(zh=along_z(j), y=mate, c=k))
    greet(partner)
    greet(dev(y=mate, c=1 - c))
    greet(dev(y=near))
    greet(dev(y=near, c=1 - c))
    for j in range(1, NL):
        greet(along_l(j))
    for j in range(1, NP):
        greet(piece(j)[1])
    pl.semaphore_wait(barrier, 2 * NC * NB + 4 + (NL - 1) + (NP - 1))

    send(wt.at[:, :, half_at(1 - c)], w2.at[my_chunks], wp_send, wp_recv, partner)
    w_own.wait()
    await_bytes(w2.at[my_chunks], wp_recv)
    def s10(q):
        for j, sem in (UP, wu_recv), (DOWN, wd_recv):
            send(
                w2.at[q],
                g.at[q, 0, b, SLOT[NZ - j]],
                w_send.at[q],
                sem.at[q],
                dev(zh=along_z(j), y=yt, c=b),
            )

    for stage, q in STEPS[:LEAD]:
        s10(q)
    w_here = jnp.logical_and(yt == y, b == c)
    put(w2, g.at[:, 0, b, 0], wo_send, wo_recv, dev(y=yt, c=b), w_here)
    a_here = b == c
    put(calib.at[:, half_at(h)], a.at[my_rows], ao_send, a_recv, dev(c=b), a_here)
    send(
        calib.at[:, half_at(1 - h)], a.at[my_rows], an_send, a_recv, dev(y=mate, c=b)
    )

    ways = ((UP, pl.ds(0, cut)), (DOWN, pl.ds(cut, half - cut)))

    def s8(q):
        for (j, lanes), sem in zip(ways, (wu_recv, wd_recv)):
            got = g.at[q, 0, c, SLOT[NZ - j]]
            await_bytes(got, sem.at[q])
            send(
                got.at[:, lanes],
                g.at[q, 0, c, SLOT[FAR], :, lanes],
                wr_send.at[q],
                wr_recv.at[q],
                dev(zh=along_z(j)),
            )
        if q == first(8):
            await_bytes(w2, wo_recv)
        got = g.at[q, 0, c, most]
        send(got, g.at[q, 1, c, most], gy_send.at[q], gy_recv.at[q], dev(y=near))
        send(got, got, gp_send.at[q], gp_recv.at[q], partner)

    def s0(q):
        got = g.at[q, 0, c, SLOT[FAR]]
        await_bytes(got, wr_recv.at[q])
        dst = g.at[q, 1, c, SLOT[FAR]]
        send(got, dst, gf_send.at[q], gf_recv.at[q], dev(y=near, c=1 - c))
        send(got, dst, gf_send.at[q], gf_recv.at[q], dev(y=near))
        send(got, got, gp_send.at[q], gp_recv.at[q], partner)

    def s1(q):
        got = g.at[q, 1, c, most]
        await_bytes(got, gy_recv.at[q])
        send(got, got, gb_send.at[q], gb_recv.at[q], partner)

    def s2(q):
        if q == first(2):
            await_bytes(a, a_recv)
            hi, lo = split(a[...])
            ah[...] = hi
            al[...] = lo
        await_bytes(g.at[q, 0, 1 - c], gp_recv.at[q])
        await_bytes(g.at[q, 1, 1 - c, most], gb_recv.at[q])
        await_bytes(g.at[q, 1, :, SLOT[FAR]], gf_recv.at[q])
        w = split(g[q].reshape(NY * NZ * SUB, half))
        acc = dot3((ah[...], al[...]), w, ((1,), (1,)))
        p[q] = acc.reshape(p.shape[1:])

        for j in FARTHEST:
            t, to = piece(j)
            send(p.at[q, t], rs.at[q, j - 1], rs_send.at[q], rs_recv.at[q], to)

    def s3(q):
        await_bytes(rs.at[q], rs_recv.at[q])
        acc = p[q, pm]
        for j in range(NP - 1):
            acc = acc + rs[q, j]
        zx[q, zl] = acc
        for j in range(NL - 1, 0, -1):
            send(zx.at[q, zl], zx.at[q, zl], zx_send.at[q], zx_recv.at[q], along_l(j))

    def s4(q):
        await_bytes(zx.at[q, pl.ds(0, NL - 1)], zx_recv.at[q])
        acc = zx[q, 0]
        for j in range(1, NL):
            acc = acc + zx[q, j]
        m[q, pm] = acc * factor

        for j in FARTHEST:
            send(m.at[q, pm], m.at[q, pm], m_send.at[q], m_recv.at[q], piece(j)[1])

    def s5(q):
        await_bytes(m.at[q, pl.ds(0, NP - 1)], m_recv.at[q])
        v = split(m[q].reshape(NC * rows, NY * NZ * SUB))
        acc = dot3(v, (ah[...], al[...]), ((0,), (0,)))
        yo[q] = acc.reshape(yo.shape[1:])
        send(yo.at[q, :, 1 - c], yp.at[q], yp_send.at[q], yp_recv.at[q], partner)

    def s6(q):
        await_bytes(yp.at[q], yp_recv.at[q])
        y1[q] = yo[q, 1, c] + yp[q, 1]
        send(y1.at[q], yr.at[q], yr_send.at[q], yr_recv.at[q], dev(y=near))

    def s7(q):
        await_bytes(yr.at[q], yr_recv.at[q])
        rz[q] = yo[q, 0, c] + yp[q, 0] + yr[q]
        for j, lanes in ways:
            send(
                rz.at[q, SLOT[FAR], :, lanes],
                rl.at[q, :, lanes],
                rl_send.at[q],
                rl_recv.at[q],
                dev(zh=along_z(j)),
            )
        for j, lanes in ways:
            deliver(q, NZ - j, lanes)
        put(
            rz.at[q, 0],
            zr.at[q % per, 3 * h],
            zo_send.at[q],
            zr_recv.at[q % per],
            dev(y=yc, c=q // per),
            jnp.logical_and(yc == y, c == q // per),
        )

    def deliver(q, d, lanes):
        send(
            rz.at[q, SLOT[d], :, lanes],
            zr.at[q % per, 3 * h + SLOT[d], :, lanes],
            zr_send.at[q],
            zr_recv.at[q % per],
            dev(zh=along_z(d), y=yc, c=q // per),
        )

    def s9(q):
        await_bytes(rl.at[q], rl_recv.at[q])
        for j, lanes in ways:
            rz[q, SLOT[j], :, lanes] = rz[q, SLOT[j], :, lanes] + rl[q, :, lanes]
            deliver(q, j, lanes)

    for stage, q in STEPS[LEAD:]:
        (s0, s1, s2, s3, s4, s5, s6, s7, s8, s9, s10)[stage](q)

    for i in range(per):
        await_bytes(zr.at[i], zr_recv.at[i])
        for k in range(2):
            acc = zr[i, 3 * k]
            for d in range(1, 3):
                acc = acc + zr[i, 3 * k + d]
            out[i * SUB : (i + 1) * SUB, k * half : (k + 1) * half] = acc

    await_bytes(w2.at[my_chunks], wp_send)
    await_bytes(a.at[my_rows], an_send)

    @pl.when(jnp.logical_not(a_here))
    def _():
        await_bytes(a.at[my_rows], ao_send)

    @pl.when(jnp.logical_not(w_here))
    def _():
        await_bytes(w2, wo_send)

    for q in range(chunks):
        await_bytes(g.at[q, 0, 0, pl.ds(0, 2)], w_send.at[q])
        await_bytes(g.at[q, 0, 0, 0], wr_send.at[q])
        await_bytes(rl.at[q], rl_send.at[q])
        await_bytes(g.at[q, 0, 0], gp_send.at[q])
        await_bytes(g.at[q, 0, 0, most], gy_send.at[q])
        await_bytes(g.at[q, 0, 0, most], gb_send.at[q])
        await_bytes(g.at[q, 1, :, SLOT[FAR]], gf_send.at[q])
        await_bytes(rs.at[q], rs_send.at[q])
        await_bytes(zx.at[q, pl.ds(0, NL - 1)], zx_send.at[q])
        await_bytes(m.at[q, pl.ds(0, NP - 1)], m_send.at[q])
        await_bytes(yp.at[q], yp_send.at[q])
        await_bytes(yr.at[q], yr_send.at[q])
        await_bytes(rz.at[q, pl.ds(0, 2)], zr_send.at[q])

        @pl.when(jnp.logical_not(jnp.logical_and(yc == y, c == q // per)))
        def _():
            await_bytes(rz.at[q, 0], zo_send.at[q])


def shards(calib, weight):
    rows, feats = calib.shape
    wide = weight.shape[1]
    half = feats // 2
    part = NC * rows // NP
    per = wide // SUB
    q = NC * per
    f32, bf16 = jnp.float32, jnp.bfloat16
    cols = NY * NZ * SUB
    factor = 1.0 / math.sqrt(rows * lax.axis_size("tok"))
    in_hbm = lambda v: pltpu.with_memory_space_constraint(v, pltpu.HBM)
    dma = lambda *n: pltpu.SemaphoreType.DMA(n)
    return pl.pallas_call(
        functools.partial(kernel, factor),
        out_shape=jax.ShapeDtypeStruct((wide, feats), f32),
        in_specs=[pl.BlockSpec(memory_space=pl.ANY)] * 2,
        out_specs=pl.BlockSpec(memory_space=pltpu.VMEM),
        scratch_shapes=[
            pltpu.VMEM((NC * rows, half), f32),
            pltpu.VMEM((NC * rows, half), bf16),
            pltpu.VMEM((NC * rows, half), bf16),
            pltpu.VMEM((q, SUB, half), f32),
            pltpu.VMEM((q, NY // NB, NB, NZ, SUB, half), f32),
            pltpu.VMEM((q, NP, part, cols), f32),
            pltpu.VMEM((q, NP - 1, part, cols), f32),
            pltpu.VMEM((q, NL, part, cols), f32),
            pltpu.VMEM((q, NP, part, cols), f32),
            pltpu.VMEM((q, NY // NB, NB, NZ, SUB, half), f32),
            pltpu.VMEM((q, NY // NB, NZ, SUB, half), f32),
            pltpu.VMEM((q, NZ, SUB, half), f32),
            pltpu.VMEM((q, NZ, SUB, half), f32),
            pltpu.VMEM((q, NZ, SUB, half), f32),
            pltpu.VMEM((q, SUB, half), f32),
            pltpu.VMEM((per, 2 * 3, SUB, half), f32),
            *[pltpu.SemaphoreType.DMA] * 8,
            *[dma(q) for _ in range(27)],
            dma(per),
        ],
        compiler_params=pltpu.CompilerParams(
            collective_id=0, has_side_effects=True, vmem_limit_bytes=48 * 1024 * 1024
        ),
        name="gram",
    )(in_hbm(calib), in_hbm(weight.T.reshape(per, SUB, feats)))


def solution(mesh):
    return jax.shard_map(
        shards,
        mesh=mesh,
        in_specs=(P("tok", "feat"), P("feat", "tok")),
        out_specs=P("tok", "feat"),
        check_vma=False,
    )
```

```python
import functools
import math

import jax
import jax.numpy as jnp
from jax import lax
from jax.experimental import pallas as pl
from jax.experimental.pallas import tpu as pltpu
from jax.sharding import PartitionSpec as P

MESH = pl.DeviceIdType.MESH
NZ, NY, NC, NX, NL = 4, 4, 2, 4, 4
NB = 2
NP = NX * NB
UP, FAR, DOWN = 1, 2, 3
ROUND = (1, 7, 2, 6, 3, 5, 4)
SLOT = (0, 1, 3, 2)
SUB = 8
STEPS = (
    (10, 0), (10, 1), (10, 2), (10, 3), (8, 0), (8, 1), (1, 0), (8, 2),
    (0, 0), (8, 3), (1, 1), (0, 1), (2, 0), (1, 2), (0, 2), (2, 1),
    (1, 3), (0, 3), (2, 2), (3, 0), (2, 3), (3, 1), (4, 0), (3, 2),
    (4, 1), (5, 0), (3, 3), (4, 2), (6, 0), (5, 1), (4, 3), (6, 1),
    (5, 2), (6, 2), (11, 0), (7, 0), (5, 3), (11, 1), (6, 3), (11, 2),
    (7, 1), (9, 0), (11, 3), (7, 2), (7, 3), (9, 1), (9, 2), (9, 3),
)


def first(stage):
    return next(q for s, q in STEPS if s == stage)


LEAD = sum(1 for k, s in enumerate(STEPS) if all(t[0] == 10 for t in STEPS[: k + 1]))


def split(v):
    hi = v.astype(jnp.bfloat16)
    return hi, (v - hi.astype(jnp.float32)).astype(jnp.bfloat16)


def dot3(a, b, dims):
    (ah, al), (bh, bl) = a, b
    f = lambda p, q: lax.dot_general(
        p, q, (dims, ((), ())), preferred_element_type=jnp.float32
    )
    return f(ah, bh) + (f(ah, bl) + f(al, bh))


def kernel(
    factor,
    calib,
    wt,
    out,
    a,
    ah,
    al,
    w2,
    g,
    p,
    rs,
    zx,
    m,
    yo,
    yp,
    y1,
    yr,
    rz,
    rl,
    zr,
    loc_sem,
    wp_send,
    wp_recv,
    ao_send,
    an_send,
    a_recv,
    wo_send,
    wo_recv,
    w_send,
    wu_recv,
    wd_recv,
    wr_send,
    wr_recv,
    gp_send,
    gp_recv,
    gy_send,
    gy_recv,
    gb_send,
    gb_recv,
    gf_send,
    gf_recv,
    rs_send,
    rs_recv,
    zx_send,
    zx_recv,
    m_send,
    m_recv,
    yp_send,
    yp_recv,
    yf_send,
    yf_recv,
    yr_send,
    yr_recv,
    zr_send,
    zo_send,
    rl_send,
    rl_recv,
    zr_recv,
):
    tok, feat = lax.axis_index("tok"), lax.axis_index("feat")
    zh, y, c = tok // (NY * NC), lax.rem(tok, NY * NC) // NC, lax.rem(tok, NC)
    x, zl = feat // NL, lax.rem(feat, NL)
    b, pair = lax.rem(y, NB), y // NB
    h = lax.rem(b + pair, 2)
    mate = pair * NB + 1 - b
    near = NY - 1 - y
    yc = pair * NB + c
    yt = jnp.where(h == c, y, mate)
    pm = x * NB + b
    half = calib.shape[1] // 2
    rows = calib.shape[0]
    cut = half // 256 * 128 + 128
    per = wt.shape[0]
    chunks = NC * per

    def dev(zh=zh, y=y, c=c, x=x, zl=zl):
        return ((zh * NY + y) * NC + c, x * NL + zl)

    def along_z(j):
        return lax.rem(zh + j, NZ)

    def along_l(j):
        low = zl < NL // 2
        to = (
            jnp.where(low, 1 - zl, 2 * NL - 3 - zl),
            jnp.where(low, NL - 2, 1),
            jnp.where(low, NL - 1, 0),
        )
        return dev(zl=to[j - 1])

    def piece(j):
        t = lax.rem(pm + j, NP)
        return t, dev(x=t // NB, y=pair * NB + lax.rem(t, NB))

    partner = dev(c=1 - c)

    def send(src, dst, ssem, rsem, to):
        pltpu.make_async_remote_copy(
            src_ref=src,
            dst_ref=dst,
            send_sem=ssem,
            recv_sem=rsem,
            device_id=to,
            device_id_type=MESH,
        ).start()

    def put(src, dst, ssem, rsem, to, here):
        @pl.when(here)
        def _():
            pltpu.make_async_copy(src, dst, rsem).start()

        @pl.when(jnp.logical_not(here))
        def _():
            send(src, dst, ssem, rsem, to)

    def await_bytes(ref, sem):
        pltpu.make_async_copy(ref, ref, sem).wait()

    def half_at(k):
        return pl.ds(pl.multiple_of(k * half, 128), half)

    my_rows = pl.ds(pl.multiple_of(c * rows, 8), rows)
    my_chunks = pl.ds(c * per, per)
    most = pl.ds(0, NZ - 1)

    w_own = pltpu.make_async_copy(wt.at[:, :, half_at(c)], w2.at[my_chunks], loc_sem)
    w_own.start()

    barrier = pltpu.get_barrier_semaphore()

    def greet(to):
        pl.semaphore_signal(barrier, inc=1, device_id=to, device_id_type=MESH)

    for j in (1, NZ - 1):
        for k in range(NC):
            greet(dev(zh=along_z(j), c=k))
            greet(dev(zh=along_z(j), y=mate, c=k))
    greet(partner)
    greet(dev(y=mate, c=1 - c))
    greet(dev(y=near))
    greet(dev(y=near, c=1 - c))
    for j in range(1, NL):
        greet(along_l(j))
    for j in range(1, NP):
        greet(piece(j)[1])
    pl.semaphore_wait(barrier, 2 * NC * NB + 4 + (NL - 1) + (NP - 1))

    send(wt.at[:, :, half_at(1 - c)], w2.at[my_chunks], wp_send, wp_recv, partner)
    w_own.wait()
    await_bytes(w2.at[my_chunks], wp_recv)
    def s10(q):
        for j, sem in (UP, wu_recv), (DOWN, wd_recv):
            send(
                w2.at[q],
                g.at[q, 0, b, SLOT[NZ - j]],
                w_send.at[q],
                sem.at[q],
                dev(zh=along_z(j), y=yt, c=b),
            )

    for stage, q in STEPS[:LEAD]:
        s10(q)
    w_here = jnp.logical_and(yt == y, b == c)
    put(w2, g.at[:, 0, b, 0], wo_send, wo_recv, dev(y=yt, c=b), w_here)
    a_here = b == c
    put(calib.at[:, half_at(h)], a.at[my_rows], ao_send, a_recv, dev(c=b), a_here)
    send(
        calib.at[:, half_at(1 - h)], a.at[my_rows], an_send, a_recv, dev(y=mate, c=b)
    )

    ways = ((UP, pl.ds(0, cut)), (DOWN, pl.ds(cut, half - cut)))

    def s8(q):
        for (j, lanes), sem in zip(ways, (wu_recv, wd_recv)):
            got = g.at[q, 0, c, SLOT[NZ - j]]
            await_bytes(got, sem.at[q])
            send(
                got.at[:, lanes],
                g.at[q, 0, c, SLOT[FAR], :, lanes],
                wr_send.at[q],
                wr_recv.at[q],
                dev(zh=along_z(j)),
            )
        if q == first(8):
            await_bytes(w2, wo_recv)
        got = g.at[q, 0, c, most]
        send(got, g.at[q, 1, c, most], gy_send.at[q], gy_recv.at[q], dev(y=near))
        send(got, got, gp_send.at[q], gp_recv.at[q], partner)

    def s0(q):
        got = g.at[q, 0, c, SLOT[FAR]]
        await_bytes(got, wr_recv.at[q])
        dst = g.at[q, 1, c, SLOT[FAR]]
        send(got, dst, gf_send.at[q], gf_recv.at[q], dev(y=near, c=1 - c))
        send(got, dst, gf_send.at[q], gf_recv.at[q], dev(y=near))
        send(got, got, gp_send.at[q], gp_recv.at[q], partner)

    def s1(q):
        got = g.at[q, 1, c, most]
        await_bytes(got, gy_recv.at[q])
        send(got, got, gb_send.at[q], gb_recv.at[q], partner)

    def s2(q):
        if q == first(2):
            await_bytes(a, a_recv)
            hi, lo = split(a[...])
            ah[...] = hi
            al[...] = lo
        await_bytes(g.at[q, 0, 1 - c], gp_recv.at[q])
        await_bytes(g.at[q, 1, 1 - c, most], gb_recv.at[q])
        await_bytes(g.at[q, 1, :, SLOT[FAR]], gf_recv.at[q])
        w = split(g[q].reshape(NY * NZ * SUB, half))
        acc = dot3((ah[...], al[...]), w, ((1,), (1,)))
        p[q] = acc.reshape(p.shape[1:])

        for j in ROUND:
            t, to = piece(j)
            send(p.at[q, t], rs.at[q, j - 1], rs_send.at[q], rs_recv.at[q], to)

    def s3(q):
        await_bytes(rs.at[q], rs_recv.at[q])
        acc = p[q, pm]
        for j in range(NP - 1):
            acc = acc + rs[q, j]
        zx[q, zl] = acc
        for j in range(NL - 1, 0, -1):
            send(zx.at[q, zl], zx.at[q, zl], zx_send.at[q], zx_recv.at[q], along_l(j))

    def s4(q):
        await_bytes(zx.at[q, pl.ds(0, NL - 1)], zx_recv.at[q])
        acc = zx[q, 0]
        for j in range(1, NL):
            acc = acc + zx[q, j]
        m[q, pm] = acc * factor

        for j in ROUND:
            send(m.at[q, pm], m.at[q, pm], m_send.at[q], m_recv.at[q], piece(j)[1])

    def s5(q):
        await_bytes(m.at[q, pl.ds(0, NP - 1)], m_recv.at[q])
        v = split(m[q].reshape(NC * rows, NY * NZ * SUB))
        acc = dot3(v, (ah[...], al[...]), ((0,), (0,)))
        yo[q] = acc.reshape(yo.shape[1:])
        send(yo.at[q, :, 1 - c], yp.at[q], yp_send.at[q], yp_recv.at[q], partner)

    def s6(q):
        await_bytes(yp.at[q], yp_recv.at[q])
        y1[q] = yo[q, 1, c] + yp[q, 1]
        far, to = SLOT[FAR], dev(y=near)
        send(y1.at[q, far], yr.at[q, far], yf_send.at[q], yf_recv.at[q], to)
        send(y1.at[q, most], yr.at[q, most], yr_send.at[q], yr_recv.at[q], to)

    def s11(q):
        far = SLOT[FAR]
        await_bytes(yr.at[q, far], yf_recv.at[q])
        rz[q, far] = yo[q, 0, c, far] + yp[q, 0, far] + yr[q, far]
        for j, lanes in ways:
            send(
                rz.at[q, far, :, lanes],
                rl.at[q, :, lanes],
                rl_send.at[q],
                rl_recv.at[q],
                dev(zh=along_z(j)),
            )

    def s7(q):
        await_bytes(yr.at[q, most], yr_recv.at[q])
        rz[q, most] = yo[q, 0, c, most] + yp[q, 0, most] + yr[q, most]
        for j, lanes in ways:
            deliver(q, NZ - j, lanes)
        put(
            rz.at[q, 0],
            zr.at[q % per, 3 * h],
            zo_send.at[q],
            zr_recv.at[q % per],
            dev(y=yc, c=q // per),
            jnp.logical_and(yc == y, c == q // per),
        )

    def deliver(q, d, lanes):
        send(
            rz.at[q, SLOT[d], :, lanes],
            zr.at[q % per, 3 * h + SLOT[d], :, lanes],
            zr_send.at[q],
            zr_recv.at[q % per],
            dev(zh=along_z(d), y=yc, c=q // per),
        )

    def s9(q):
        await_bytes(rl.at[q], rl_recv.at[q])
        for j, lanes in ways:
            rz[q, SLOT[j], :, lanes] = rz[q, SLOT[j], :, lanes] + rl[q, :, lanes]
            deliver(q, j, lanes)

    for stage, q in STEPS[LEAD:]:
        (s0, s1, s2, s3, s4, s5, s6, s7, s8, s9, s10, s11)[stage](q)

    for i in range(per):
        await_bytes(zr.at[i], zr_recv.at[i])
        for k in range(2):
            acc = zr[i, 3 * k]
            for d in range(1, 3):
                acc = acc + zr[i, 3 * k + d]
            out[i * SUB : (i + 1) * SUB, k * half : (k + 1) * half] = acc

    await_bytes(w2.at[my_chunks], wp_send)
    await_bytes(a.at[my_rows], an_send)

    @pl.when(jnp.logical_not(a_here))
    def _():
        await_bytes(a.at[my_rows], ao_send)

    @pl.when(jnp.logical_not(w_here))
    def _():
        await_bytes(w2, wo_send)

    for q in range(chunks):
        await_bytes(g.at[q, 0, 0, pl.ds(0, 2)], w_send.at[q])
        await_bytes(g.at[q, 0, 0, 0], wr_send.at[q])
        await_bytes(rl.at[q], rl_send.at[q])
        await_bytes(g.at[q, 0, 0], gp_send.at[q])
        await_bytes(g.at[q, 0, 0, most], gy_send.at[q])
        await_bytes(g.at[q, 0, 0, most], gb_send.at[q])
        await_bytes(g.at[q, 1, :, SLOT[FAR]], gf_send.at[q])
        await_bytes(rs.at[q], rs_send.at[q])
        await_bytes(zx.at[q, pl.ds(0, NL - 1)], zx_send.at[q])
        await_bytes(m.at[q, pl.ds(0, NP - 1)], m_send.at[q])
        await_bytes(yp.at[q], yp_send.at[q])
        await_bytes(yr.at[q, SLOT[FAR]], yf_send.at[q])
        await_bytes(yr.at[q, most], yr_send.at[q])
        await_bytes(rz.at[q, pl.ds(0, 2)], zr_send.at[q])

        @pl.when(jnp.logical_not(jnp.logical_and(yc == y, c == q // per)))
        def _():
            await_bytes(rz.at[q, 0], zo_send.at[q])


def shards(calib, weight):
    rows, feats = calib.shape
    wide = weight.shape[1]
    half = feats // 2
    part = NC * rows // NP
    per = wide // SUB
    q = NC * per
    f32, bf16 = jnp.float32, jnp.bfloat16
    cols = NY * NZ * SUB
    factor = 1.0 / math.sqrt(rows * lax.axis_size("tok"))
    in_hbm = lambda v: pltpu.with_memory_space_constraint(v, pltpu.HBM)
    dma = lambda *n: pltpu.SemaphoreType.DMA(n)
    return pl.pallas_call(
        functools.partial(kernel, factor),
        out_shape=jax.ShapeDtypeStruct((wide, feats), f32),
        in_specs=[pl.BlockSpec(memory_space=pl.ANY)] * 2,
        out_specs=pl.BlockSpec(memory_space=pltpu.VMEM),
        scratch_shapes=[
            pltpu.VMEM((NC * rows, half), f32),
            pltpu.VMEM((NC * rows, half), bf16),
            pltpu.VMEM((NC * rows, half), bf16),
            pltpu.VMEM((q, SUB, half), f32),
            pltpu.VMEM((q, NY // NB, NB, NZ, SUB, half), f32),
            pltpu.VMEM((q, NP, part, cols), f32),
            pltpu.VMEM((q, NP - 1, part, cols), f32),
            pltpu.VMEM((q, NL, part, cols), f32),
            pltpu.VMEM((q, NP, part, cols), f32),
            pltpu.VMEM((q, NY // NB, NB, NZ, SUB, half), f32),
            pltpu.VMEM((q, NY // NB, NZ, SUB, half), f32),
            pltpu.VMEM((q, NZ, SUB, half), f32),
            pltpu.VMEM((q, NZ, SUB, half), f32),
            pltpu.VMEM((q, NZ, SUB, half), f32),
            pltpu.VMEM((q, SUB, half), f32),
            pltpu.VMEM((per, 2 * 3, SUB, half), f32),
            *[pltpu.SemaphoreType.DMA] * 8,
            *[dma(q) for _ in range(29)],
            dma(per),
        ],
        compiler_params=pltpu.CompilerParams(
            collective_id=0, has_side_effects=True, vmem_limit_bytes=48 * 1024 * 1024
        ),
        name="gram",
    )(in_hbm(calib), in_hbm(weight.T.reshape(per, SUB, feats)))


def solution(mesh):
    return jax.shard_map(
        shards,
        mesh=mesh,
        in_specs=(P("tok", "feat"), P("feat", "tok")),
        out_specs=P("tok", "feat"),
        check_vma=False,
    )
```

```python
import functools
import math

import jax
import jax.numpy as jnp
from jax import lax
from jax.experimental import pallas as pl
from jax.experimental.pallas import tpu as pltpu
from jax.sharding import PartitionSpec as P

MESH = pl.DeviceIdType.MESH
NZ, NY, NC, NX, NL = 4, 4, 2, 4, 4
NB = 2
NP = NX * NB
UP, FAR, DOWN = 1, 2, 3
ROUND = (1, 7, 2, 6, 3, 5, 4)
SLOT = (0, 1, 3, 2)
SUB = 8
STEPS = (
    (10, 0), (10, 1), (10, 2), (10, 3), (8, 0), (8, 1), (1, 0), (8, 2),
    (0, 0), (8, 3), (1, 1), (0, 1), (2, 0), (1, 2), (0, 2), (2, 1),
    (1, 3), (0, 3), (2, 2), (3, 0), (2, 3), (3, 1), (4, 0), (3, 2),
    (4, 1), (5, 0), (3, 3), (4, 2), (6, 0), (5, 1), (4, 3), (6, 1),
    (5, 2), (6, 2), (11, 0), (7, 0), (5, 3), (11, 1), (6, 3), (11, 2),
    (7, 1), (9, 0), (11, 3), (7, 2), (7, 3), (9, 1), (9, 2), (9, 3),
)


def first(stage):
    return next(q for s, q in STEPS if s == stage)


LEAD = sum(1 for k, s in enumerate(STEPS) if all(t[0] == 10 for t in STEPS[: k + 1]))


def split(v):
    hi = v.astype(jnp.bfloat16)
    return hi, (v - hi.astype(jnp.float32)).astype(jnp.bfloat16)


def dot3(a, b, dims):
    (ah, al), (bh, bl) = a, b
    f = lambda p, q: lax.dot_general(
        p, q, (dims, ((), ())), preferred_element_type=jnp.float32
    )
    return f(ah, bh) + (f(ah, bl) + f(al, bh))


def kernel(
    factor,
    calib,
    wt,
    out,
    a,
    ah,
    al,
    w2,
    g,
    p,
    rs,
    zx,
    m,
    yo,
    yp,
    y1,
    yr,
    rz,
    rl,
    zr,
    loc_sem,
    wp_send,
    wp_recv,
    ao_send,
    an_send,
    a_recv,
    wo_send,
    wo_recv,
    w_send,
    wu_recv,
    wd_recv,
    wr_send,
    wr_recv,
    gp_send,
    gp_recv,
    gy_send,
    gy_recv,
    gb_send,
    gb_recv,
    gf_send,
    gf_recv,
    rs_send,
    rs_recv,
    zx_send,
    zx_recv,
    m_send,
    m_recv,
    yp_send,
    yp_recv,
    yf_send,
    yf_recv,
    yr_send,
    yr_recv,
    zr_send,
    zo_send,
    rl_send,
    rl_recv,
    zr_recv,
):
    tok, feat = lax.axis_index("tok"), lax.axis_index("feat")
    zh, y, c = tok // (NY * NC), lax.rem(tok, NY * NC) // NC, lax.rem(tok, NC)
    x, zl = feat // NL, lax.rem(feat, NL)
    b, pair = lax.rem(y, NB), y // NB
    h = lax.rem(b + pair, 2)
    mate = pair * NB + 1 - b
    near = NY - 1 - y
    yc = pair * NB + c
    yt = jnp.where(h == c, y, mate)
    pm = x * NB + b
    half = calib.shape[1] // 2
    rows = calib.shape[0]
    cut = half // 256 * 128 + 128
    per = wt.shape[0]
    chunks = NC * per

    def dev(zh=zh, y=y, c=c, x=x, zl=zl):
        return ((zh * NY + y) * NC + c, x * NL + zl)

    def along_z(j):
        return lax.rem(zh + j, NZ)

    def along_l(j):
        low = zl < NL // 2
        to = (
            jnp.where(low, 1 - zl, 2 * NL - 3 - zl),
            jnp.where(low, NL - 2, 1),
            jnp.where(low, NL - 1, 0),
        )
        return dev(zl=to[j - 1])

    def piece(j):
        t = lax.rem(pm + j, NP)
        return t, dev(x=t // NB, y=pair * NB + lax.rem(t, NB))

    partner = dev(c=1 - c)

    def send(src, dst, ssem, rsem, to):
        pltpu.make_async_remote_copy(
            src_ref=src,
            dst_ref=dst,
            send_sem=ssem,
            recv_sem=rsem,
            device_id=to,
            device_id_type=MESH,
        ).start()

    def put(src, dst, ssem, rsem, to, here):
        @pl.when(here)
        def _():
            pltpu.make_async_copy(src, dst, rsem).start()

        @pl.when(jnp.logical_not(here))
        def _():
            send(src, dst, ssem, rsem, to)

    def await_bytes(ref, sem):
        pltpu.make_async_copy(ref, ref, sem).wait()

    def half_at(k):
        return pl.ds(pl.multiple_of(k * half, 128), half)

    my_rows = pl.ds(pl.multiple_of(c * rows, 8), rows)
    my_chunks = pl.ds(c * per, per)
    most = pl.ds(0, NZ - 1)

    w_own = pltpu.make_async_copy(wt.at[:, :, half_at(c)], w2.at[my_chunks], loc_sem)
    w_own.start()

    barrier = pltpu.get_barrier_semaphore()

    def greet(to):
        pl.semaphore_signal(barrier, inc=1, device_id=to, device_id_type=MESH)

    for j in (1, NZ - 1):
        for k in range(NC):
            greet(dev(zh=along_z(j), c=k))
            greet(dev(zh=along_z(j), y=mate, c=k))
    greet(partner)
    greet(dev(y=mate, c=1 - c))
    greet(dev(y=near))
    greet(dev(y=near, c=1 - c))
    for j in range(1, NL):
        greet(along_l(j))
    for j in range(1, NP):
        greet(piece(j)[1])
    pl.semaphore_wait(barrier, 2 * NC * NB + 4 + (NL - 1) + (NP - 1))

    send(wt.at[:, :, half_at(1 - c)], w2.at[my_chunks], wp_send, wp_recv, partner)
    w_own.wait()
    await_bytes(w2.at[my_chunks], wp_recv)
    def s10(q):
        for j, sem in (UP, wu_recv), (DOWN, wd_recv):
            send(
                w2.at[q],
                g.at[q, 0, b, SLOT[NZ - j]],
                w_send.at[q],
                sem.at[q],
                dev(zh=along_z(j), y=yt, c=b),
            )

    for stage, q in STEPS[:LEAD]:
        s10(q)
    w_here = jnp.logical_and(yt == y, b == c)
    put(w2, g.at[:, 0, b, 0], wo_send, wo_recv, dev(y=yt, c=b), w_here)
    a_here = b == c
    put(calib.at[:, half_at(h)], a.at[my_rows], ao_send, a_recv, dev(c=b), a_here)
    send(
        calib.at[:, half_at(1 - h)], a.at[my_rows], an_send, a_recv, dev(y=mate, c=b)
    )

    ways = ((UP, pl.ds(0, cut)), (DOWN, pl.ds(cut, half - cut)))

    def s8(q):
        for (j, lanes), sem in zip(ways, (wu_recv, wd_recv)):
            got = g.at[q, 0, c, SLOT[NZ - j]]
            await_bytes(got, sem.at[q])
            send(
                got.at[:, lanes],
                g.at[q, 0, c, SLOT[FAR], :, lanes],
                wr_send.at[q],
                wr_recv.at[q],
                dev(zh=along_z(j)),
            )
        if q == first(8):
            await_bytes(w2, wo_recv)
        got = g.at[q, 0, c, most]
        send(got, g.at[q, 1, c, most], gy_send.at[q], gy_recv.at[q], dev(y=near))
        send(got, got, gp_send.at[q], gp_recv.at[q], partner)

    def s0(q):
        got = g.at[q, 0, c, SLOT[FAR]]
        await_bytes(got, wr_recv.at[q])
        dst = g.at[q, 1, c, SLOT[FAR]]
        send(got, dst, gf_send.at[q], gf_recv.at[q], dev(y=near, c=1 - c))
        send(got, dst, gf_send.at[q], gf_recv.at[q], dev(y=near))
        send(got, got, gp_send.at[q], gp_recv.at[q], partner)

    def s1(q):
        got = g.at[q, 1, c, most]
        await_bytes(got, gy_recv.at[q])
        send(got, got, gb_send.at[q], gb_recv.at[q], partner)

    def s2(q):
        if q == first(2):
            await_bytes(a, a_recv)
            hi, lo = split(a[...])
            ah[...] = hi
            al[...] = lo
        await_bytes(g.at[q, 0, 1 - c], gp_recv.at[q])
        await_bytes(g.at[q, 1, 1 - c, most], gb_recv.at[q])
        await_bytes(g.at[q, 1, :, SLOT[FAR]], gf_recv.at[q])
        w = split(g[q].reshape(NY * NZ * SUB, half))
        acc = dot3((ah[...], al[...]), w, ((1,), (1,)))
        p[q] = acc.reshape(p.shape[1:])

        for j in ROUND:
            t, to = piece(j)
            send(p.at[q, t], rs.at[q, j - 1], rs_send.at[q], rs_recv.at[q], to)

    def s3(q):
        await_bytes(rs.at[q], rs_recv.at[q])
        acc = p[q, pm]
        for j in range(NP - 1):
            acc = acc + rs[q, j]
        zx[q, zl] = acc
        for j in range(NL - 1, 0, -1):
            send(zx.at[q, zl], zx.at[q, zl], zx_send.at[q], zx_recv.at[q], along_l(j))

    def s4(q):
        await_bytes(zx.at[q, pl.ds(0, NL - 1)], zx_recv.at[q])
        acc = zx[q, 0]
        for j in range(1, NL):
            acc = acc + zx[q, j]
        m[q, pm] = acc * factor

        for j in ROUND:
            send(m.at[q, pm], m.at[q, pm], m_send.at[q], m_recv.at[q], piece(j)[1])

    def s5(q):
        await_bytes(m.at[q, pl.ds(0, NP - 1)], m_recv.at[q])
        v = split(m[q].reshape(NC * rows, NY * NZ * SUB))
        acc = dot3(v, (ah[...], al[...]), ((0,), (0,)))
        yo[q] = acc.reshape(yo.shape[1:])
        send(yo.at[q, :, 1 - c], yp.at[q], yp_send.at[q], yp_recv.at[q], partner)

    def s6(q):
        await_bytes(yp.at[q], yp_recv.at[q])
        far, to = SLOT[FAR], dev(y=near)
        y1[q, far] = yo[q, 1, c, far] + yp[q, 1, far]
        send(y1.at[q, far], yr.at[q, far], yf_send.at[q], yf_recv.at[q], to)
        y1[q, most] = yo[q, 1, c, most] + yp[q, 1, most]
        send(y1.at[q, most], yr.at[q, most], yr_send.at[q], yr_recv.at[q], to)

    def s11(q):
        far = SLOT[FAR]
        await_bytes(yr.at[q, far], yf_recv.at[q])
        rz[q, far] = yo[q, 0, c, far] + yp[q, 0, far] + yr[q, far]
        for j, lanes in ways:
            send(
                rz.at[q, far, :, lanes],
                rl.at[q, :, lanes],
                rl_send.at[q],
                rl_recv.at[q],
                dev(zh=along_z(j)),
            )

    def s7(q):
        await_bytes(yr.at[q, most], yr_recv.at[q])
        rz[q, most] = yo[q, 0, c, most] + yp[q, 0, most] + yr[q, most]
        for j, lanes in ways:
            deliver(q, NZ - j, lanes)
        put(
            rz.at[q, 0],
            zr.at[q % per, 3 * h],
            zo_send.at[q],
            zr_recv.at[q % per],
            dev(y=yc, c=q // per),
            jnp.logical_and(yc == y, c == q // per),
        )

    def deliver(q, d, lanes):
        send(
            rz.at[q, SLOT[d], :, lanes],
            zr.at[q % per, 3 * h + SLOT[d], :, lanes],
            zr_send.at[q],
            zr_recv.at[q % per],
            dev(zh=along_z(d), y=yc, c=q // per),
        )

    def s9(q):
        await_bytes(rl.at[q], rl_recv.at[q])
        for j, lanes in ways:
            rz[q, SLOT[j], :, lanes] = rz[q, SLOT[j], :, lanes] + rl[q, :, lanes]
            deliver(q, j, lanes)

    for stage, q in STEPS[LEAD:]:
        (s0, s1, s2, s3, s4, s5, s6, s7, s8, s9, s10, s11)[stage](q)

    for i in range(per):
        await_bytes(zr.at[i], zr_recv.at[i])
        for k in range(2):
            acc = zr[i, 3 * k]
            for d in range(1, 3):
                acc = acc + zr[i, 3 * k + d]
            out[i * SUB : (i + 1) * SUB, k * half : (k + 1) * half] = acc

    await_bytes(w2.at[my_chunks], wp_send)
    await_bytes(a.at[my_rows], an_send)

    @pl.when(jnp.logical_not(a_here))
    def _():
        await_bytes(a.at[my_rows], ao_send)

    @pl.when(jnp.logical_not(w_here))
    def _():
        await_bytes(w2, wo_send)

    for q in range(chunks):
        await_bytes(g.at[q, 0, 0, pl.ds(0, 2)], w_send.at[q])
        await_bytes(g.at[q, 0, 0, 0], wr_send.at[q])
        await_bytes(rl.at[q], rl_send.at[q])
        await_bytes(g.at[q, 0, 0], gp_send.at[q])
        await_bytes(g.at[q, 0, 0, most], gy_send.at[q])
        await_bytes(g.at[q, 0, 0, most], gb_send.at[q])
        await_bytes(g.at[q, 1, :, SLOT[FAR]], gf_send.at[q])
        await_bytes(rs.at[q], rs_send.at[q])
        await_bytes(zx.at[q, pl.ds(0, NL - 1)], zx_send.at[q])
        await_bytes(m.at[q, pl.ds(0, NP - 1)], m_send.at[q])
        await_bytes(yp.at[q], yp_send.at[q])
        await_bytes(yr.at[q, SLOT[FAR]], yf_send.at[q])
        await_bytes(yr.at[q, most], yr_send.at[q])
        await_bytes(rz.at[q, pl.ds(0, 2)], zr_send.at[q])

        @pl.when(jnp.logical_not(jnp.logical_and(yc == y, c == q // per)))
        def _():
            await_bytes(rz.at[q, 0], zo_send.at[q])


def shards(calib, weight):
    rows, feats = calib.shape
    wide = weight.shape[1]
    half = feats // 2
    part = NC * rows // NP
    per = wide // SUB
    q = NC * per
    f32, bf16 = jnp.float32, jnp.bfloat16
    cols = NY * NZ * SUB
    factor = 1.0 / math.sqrt(rows * lax.axis_size("tok"))
    in_hbm = lambda v: pltpu.with_memory_space_constraint(v, pltpu.HBM)
    dma = lambda *n: pltpu.SemaphoreType.DMA(n)
    return pl.pallas_call(
        functools.partial(kernel, factor),
        out_shape=jax.ShapeDtypeStruct((wide, feats), f32),
        in_specs=[pl.BlockSpec(memory_space=pl.ANY)] * 2,
        out_specs=pl.BlockSpec(memory_space=pltpu.VMEM),
        scratch_shapes=[
            pltpu.VMEM((NC * rows, half), f32),
            pltpu.VMEM((NC * rows, half), bf16),
            pltpu.VMEM((NC * rows, half), bf16),
            pltpu.VMEM((q, SUB, half), f32),
            pltpu.VMEM((q, NY // NB, NB, NZ, SUB, half), f32),
            pltpu.VMEM((q, NP, part, cols), f32),
            pltpu.VMEM((q, NP - 1, part, cols), f32),
            pltpu.VMEM((q, NL, part, cols), f32),
            pltpu.VMEM((q, NP, part, cols), f32),
            pltpu.VMEM((q, NY // NB, NB, NZ, SUB, half), f32),
            pltpu.VMEM((q, NY // NB, NZ, SUB, half), f32),
            pltpu.VMEM((q, NZ, SUB, half), f32),
            pltpu.VMEM((q, NZ, SUB, half), f32),
            pltpu.VMEM((q, NZ, SUB, half), f32),
            pltpu.VMEM((q, SUB, half), f32),
            pltpu.VMEM((per, 2 * 3, SUB, half), f32),
            *[pltpu.SemaphoreType.DMA] * 8,
            *[dma(q) for _ in range(29)],
            dma(per),
        ],
        compiler_params=pltpu.CompilerParams(
            collective_id=0, has_side_effects=True, vmem_limit_bytes=48 * 1024 * 1024
        ),
        name="gram",
    )(in_hbm(calib), in_hbm(weight.T.reshape(per, SUB, feats)))


def solution(mesh):
    return jax.shard_map(
        shards,
        mesh=mesh,
        in_specs=(P("tok", "feat"), P("feat", "tok")),
        out_specs=P("tok", "feat"),
        check_vma=False,
    )
```
